768 devices in a mesh: az: 96 (over y, z_lo, core), rad: 8 (over x, z_hi).
Axes of the slice: x: 4, y: 8, z: 12 (z_hi: 2, z_lo: 6; z = z_hi * 6 + z_lo), core: 2. Of those that a mesh axis runs over, the one named last changes fastest.
Arguments:
- density: float32 [4, 1536, 1024], P(None, 'az', 'rad'), may hold values from 1 to 2
- momentum: float32 [3, 4, 1536, 1024], P(None, None, 'az', 'rad'), may hold values from -2.5 to 2.5
- magnetic: float32 [3, 4, 1536, 1024], P(None, None, 'az', 'rad'), may hold values from -3 to 3
- tracer: float32 [4, 1536, 1024], P(None, 'az', 'rad'), may hold values from 0 to 1
- shear_offset: int32 [2], replicated, may hold values from 0 to 783, as said below
Outputs:
- new_state: float32 [8, 4, 1536, 1024], P(None, None, 'az', 'rad')
The draws below stay inside these ranges and needn't reach their ends.
Inputs may be any that keep to these rules, and one draw needn't show every extreme that they name: shear_offset[0] is below 16; shear_offset[1] is 768 plus a whole number below 16.
All inputs are finite; a program needn't handle non-finite values.
Results may differ from the reference program's by a relative error of at most 0.00002.
Values sent between devices are 32-bit elements; how exact they have to be, the bound alone decides.
A program may use at most 32 MiB of HBM per device.

```python
import jax
import jax.numpy as jnp
from jax import lax

NZ = 4
AZ_DEV = 16
NY = 1536
NX = 1024


def draw_shear_offset(key, part):
    first_key = jax.random.fold_in(key, 11)
    second_key = jax.random.fold_in(key, 23)
    first = jax.random.randint(first_key, (1,), 0, AZ_DEV, dtype=jnp.int32)
    second = jax.random.randint(second_key, (1,), 0, AZ_DEV, dtype=jnp.int32) + NY // 2
    return jnp.concatenate([first, second]).astype(jnp.int32)


def shard_levels(rng, shape, cuts, smallest, top_value):
    loudness = 1.0
    for position, shards_of in cuts:
        steps = jax.random.uniform(jax.random.fold_in(jax.random.fold_in(rng, 6), position), (shards_of,), jnp.float32, smallest / len(cuts), top_value / len(cuts))
        loudness = loudness * jnp.repeat(jnp.exp(steps), shape[position] // shards_of).reshape((-1,) + (1,) * (len(shape) - 1 - position))
    return loudness


def bell_draw(stream_key, dims, width, reach, pieces=(), held_as=jnp.bfloat16):
    loudness = shard_levels(stream_key, dims, pieces, -0.22, 0.18) if pieces else 1.0
    values = jax.random.normal(stream_key, dims, jnp.float32) * width * loudness
    return jnp.minimum(jnp.maximum(values, -reach), reach).astype(held_as)


def setup_inputs(seed: int = 0) -> dict:
    key_of = jax.random.split(jax.random.key(seed), 6)
    density = jnp.clip(1.0 + 1.0 * jax.random.uniform(key_of[0], (NZ, NY, NX), jnp.float32) ** shard_levels(key_of[0], (NZ, NY, NX), ((1, 96), (2, 8)), -0.2, 0.2), 1.0, 2.0)
    momentum = bell_draw(key_of[1], (3, NZ, NY, NX), 0.4, 2.5, ((2, 96), (3, 8)), jnp.float32)
    magnetic = bell_draw(key_of[2], (3, NZ, NY, NX), 0.8, 3.0, ((2, 96), (3, 8)), jnp.float32)
    tracer = jnp.clip(1.0 * jax.random.uniform(key_of[3], (NZ, NY, NX), jnp.float32) ** shard_levels(key_of[3], (NZ, NY, NX), ((1, 96), (2, 8)), -0.2, 0.2), 0.0, 1.0)
    shear_offset = draw_shear_offset(jax.random.fold_in(key_of[5], 71), 0)
    return {"density": density, "momentum": momentum, "magnetic": magnetic, "tracer": tracer, "shear_offset": shear_offset}


time_step = 0.025
viscosity = 0.5
sound_squared = 1.0
shear_speed = 1.0
frac_weight = 0.375


def fluxes(padded, direction):
    density_part = padded[0]
    velocity = [padded[1 + component] / density_part for component in range(3)]
    field_part = [padded[4 + component] for component in range(3)]
    pressure = sound_squared * density_part + 0.5 * (field_part[0] * field_part[0] + field_part[1] * field_part[1] + field_part[2] * field_part[2])
    normal_vel = velocity[direction]
    normal_mag = field_part[direction]
    result = [padded[1 + direction]]
    for component in range(3):
        summand = padded[1 + component] * normal_vel - field_part[component] * normal_mag
        if component == direction:
            summand = summand + pressure
        result.append(summand)
    for component in range(3):
        result.append(normal_vel * field_part[component] - normal_mag * velocity[component])
    result.append(padded[7] * normal_vel)
    return jnp.stack(result)


def offset_slice(padded, along, length, shift_by):
    return lax.slice_in_dim(padded, 3 + shift_by, 3 + shift_by + length, axis=along)


def central(padded, along, length):
    return (45.0 * (offset_slice(padded, along, length, 1) - offset_slice(padded, along, length, -1))
            - 9.0 * (offset_slice(padded, along, length, 2) - offset_slice(padded, along, length, -2))
            + (offset_slice(padded, along, length, 3) - offset_slice(padded, along, length, -3))) / 60.0


def second(padded, along, length):
    return offset_slice(padded, along, length, 1) - 2.0 * offset_slice(padded, along, length, 0) + offset_slice(padded, along, length, -1)


def tendency(row_padded, col_padded):
    row_count = row_padded.shape[2] - 6
    col_count = col_padded.shape[3] - 6
    core_rows = row_padded[:, :, 3:3 + row_count]
    vertical_pad = jnp.concatenate([core_rows[:, -3:], core_rows, core_rows[:, :3]], axis=1)
    layer_count = core_rows.shape[1]
    summed = -(central(fluxes(col_padded, 0), 3, col_count) + central(fluxes(row_padded, 1), 2, row_count)
               + central(fluxes(vertical_pad, 2), 1, layer_count))
    summed = summed + viscosity * (second(col_padded, 3, col_count) + second(row_padded, 2, row_count)
                                   + second(vertical_pad, 1, layer_count))
    return summed


def blend_rows(window, row_count, lead_weight, trail_weight, jump_sign):
    blended = lead_weight * window[:, :, :row_count] + trail_weight * window[:, :, 1:row_count + 1]
    return jnp.concatenate([blended[:2], blended[2:3] + jump_sign * shear_speed * blended[0:1], blended[3:]], axis=0)


def global_tendency(conserved, offset):
    offset = offset.astype(jnp.int32)
    inner_src = conserved[..., NX - 3:]
    outer_src = conserved[..., :3]
    inner_win = lax.dynamic_slice_in_dim(jnp.concatenate([inner_src, inner_src], axis=2), offset, NY + 1, 2)
    outer_start = (NY - 1 - offset).astype(jnp.int32)
    outer_win = lax.dynamic_slice_in_dim(jnp.concatenate([outer_src, outer_src], axis=2), outer_start, NY + 1, 2)
    inner_ghost = blend_rows(inner_win, NY, 1.0 - frac_weight, frac_weight, 1.0)
    outer_ghost = blend_rows(outer_win, NY, frac_weight, 1.0 - frac_weight, -1.0)
    col_padded = jnp.concatenate([inner_ghost, conserved, outer_ghost], axis=3)
    row_padded = jnp.concatenate([conserved[:, :, -3:], conserved, conserved[:, :, :3]], axis=2)
    return tendency(row_padded, col_padded)


def reference(density, momentum, magnetic, tracer, shear_offset):
    conserved = jnp.concatenate([density[None], momentum, magnetic, tracer[None]], axis=0)
    section_one = conserved + time_step * global_tendency(conserved, shear_offset[0])
    return 0.5 * conserved + 0.5 * (section_one + time_step * global_tendency(section_one, shear_offset[1]))
```

```python
import functools

import jax
import jax.numpy as jnp
from jax import lax
from jax.experimental import pallas as pl
from jax.experimental.pallas import tpu as pltpu
from jax.sharding import PartitionSpec as P

time_step = 0.025
viscosity = 0.5
sound_squared = 1.0
shear_speed = 1.0
frac_weight = 0.375

MESH = pl.DeviceIdType.MESH
D1 = -time_step * 45.0 / 60.0
D2 = time_step * 9.0 / 60.0
D3 = -time_step / 60.0
VISC = time_step * viscosity
lead = 1.0 - frac_weight
trail = frac_weight

Y_PREV, Y_NEXT, HL_MAIN, HL_PREV, HL_NEXT, HL_FULL, HR_MAIN, HR_NEXT, HR_PREV, HR_FULL, AZ_PREV, AZ_NEXT, SWAP = range(13)
N_COPY = 13


def flux(q, inv, pres, d):
    vel = [q[1 + i] * inv for i in range(3)]
    mag = q[4:7]
    vd, bd = vel[d], mag[d]
    out = [q[1 + d]]
    for i in range(3):
        g = q[1 + i] * vd - mag[i] * bd
        out.append(g + pres if i == d else g)
    for i in range(3):
        out.append(vd * mag[i] - bd * vel[i])
    out.append(q[7] * vd)
    return out


def aux(q):
    inv = 1.0 / q[0]
    pres = sound_squared * q[0] + 0.5 * (q[4] * q[4] + q[5] * q[5] + q[6] * q[6])
    return inv, pres


def combine(up, down):
    return D1 * (up[0] - down[0]) + D2 * (up[1] - down[1]) + D3 * (up[2] - down[2])


def lane_roll(x, shift):
    shift %= 128
    return x if shift == 0 else pltpu.roll(x, shift, x.ndim - 1)


def lanes_along(g, u):
    r = combine([lane_roll(g, -k) for k in (1, 2, 3)], [lane_roll(g, k) for k in (1, 2, 3)])
    return r + VISC * (lane_roll(u, -1) - 2.0 * u + lane_roll(u, 1))


def around(x, k):
    k %= x.shape[0]
    return x if k == 0 else jnp.concatenate([x[k:], x[:k]], axis=0)


def layers_along(g, u):
    r = combine([around(g, k) for k in (1, 2, 3)], [around(g, -k) for k in (1, 2, 3)])
    return r + VISC * (around(u, 1) - 2.0 * u + around(u, -1))


def lane_layers_along(g, u):
    r = combine([lane_roll(g, -32 * k) for k in (1, 2, 3)], [lane_roll(g, 32 * k) for k in (1, 2, 3)])
    return r + VISC * (lane_roll(u, -32) - 2.0 * u + lane_roll(u, 32))


def kernel(n_az, n_rad, half_offset, off_ref, den, mom, mag, tra, out,
           w, fy, own, bhl, bhr, az, es, sp, sq, in_sem, send, recv):
    a = lax.axis_index("az")
    r = lax.axis_index("rad")
    first = r == 0
    last = r == n_rad - 1
    edge = jnp.logical_or(first, last)
    r_up = lax.rem(r + 1, n_rad)
    r_dn = lax.rem(r + n_rad - 1, n_rad)

    def at(step):
        return lax.rem(a + step + n_az, n_az)

    def dev(step, to_r):
        return (at(step), to_r)

    barrier = pltpu.get_barrier_semaphore()

    def greet(step, to_r):
        pl.semaphore_signal(barrier, inc=1, device_id=dev(step, to_r), device_id_type=MESH)

    for step in (-1, 0, 1):
        greet(step, r_up)
        greet(step, r_dn)

    @pl.when(first)
    def _():
        greet(2, r_dn)

    @pl.when(last)
    def _():
        greet(-2, r_up)

    @pl.when(edge)
    def _():
        greet(n_az // 2, r)

    greet(1, r)
    greet(-1, r)

    rows = pl.ds(8, 16)
    loads = [
        pltpu.make_async_copy(den, w.at[0, :, rows], in_sem.at[0]),
        pltpu.make_async_copy(mom, w.at[1:4, :, rows], in_sem.at[1]),
        pltpu.make_async_copy(mag, w.at[4:7, :, rows], in_sem.at[2]),
        pltpu.make_async_copy(tra, w.at[7, :, rows], in_sem.at[3]),
    ]
    for c in loads:
        c.start()
    w[:, :, 0:2, :] = jnp.ones((8, 4, 2, 128), jnp.float32)
    w[:, :, 30:32, :] = jnp.ones((8, 4, 2, 128), jnp.float32)
    for c in loads:
        c.wait()

    lane = lax.broadcasted_iota(jnp.int32, (1, 128), 1)
    group = lane // 4
    slot_is = [lane % 32 // 4 == k for k in range(8)]
    left_half = lane % 32 < 16

    def pack(read, count):
        tiles = [jnp.zeros((count, 128), jnp.float32)] * 4
        for f in range(8):
            x = read(f)
            for z in range(4):
                moved = lane_roll(x[z], 32 * z + 4 * f)
                for t, shift in enumerate((0, 1, -1, -2)):
                    here = group == (8 * z + f + shift) % 32
                    tiles[t] = jnp.where(here, moved, tiles[t])
        return tiles

    def spread(f, hlf, hln, ln, lf, rf, rn, hrn, hrf):
        def of(k):
            return slot_is[(f + k) % 8]
        left = jnp.where(of(-2), hlf, jnp.where(of(-1), hln, jnp.where(of(0), ln, lf)))
        right = jnp.where(of(-2), rf, jnp.where(of(-1), rn, jnp.where(of(0), hrn, hrf)))
        return jnp.where(left_half, lane_roll(left, 4 * (2 - f)), lane_roll(right, 4 * (6 - f)))

    tiles = pack(lambda f: w[f, :, 8:24, :], 16)
    for t in range(4):
        own[t, 8:24, :] = tiles[t]
    az[24:40, :] = jnp.where(first, tiles[0], tiles[2])

    pl.semaphore_wait(barrier, 8 + 2 * edge.astype(jnp.int32))

    def remote(k, src, dst, step, to_r):
        return pltpu.make_async_remote_copy(
            src_ref=src, dst_ref=dst, send_sem=send.at[k], recv_sem=recv.at[k],
            device_id=dev(step, to_r), device_id_type=MESH)

    own_l, own_r = own.at[0:2, 8:24], own.at[2:4, 8:24]
    ln, rn = own.at[0], own.at[2]
    hl_main = remote(HL_MAIN, own_r, bhl.at[:, 8:24], 0, r_up)
    hr_main = remote(HR_MAIN, own_l, bhr.at[:, 24:40], 0, r_dn)
    hl_full = remote(HL_FULL, own_r, bhl.at[:, 24:40], -1, r_up)
    hr_full = remote(HR_FULL, own_l, bhr.at[:, 8:24], 1, r_dn)
    hl_prev = remote(HL_PREV, rn.at[21:24], bhl.at[0, 5:8], 1, r_up)
    hr_next = remote(HR_NEXT, ln.at[8:11], bhr.at[0, 40:43], -1, r_dn)
    hl_next_in = remote(HL_NEXT, rn.at[8:11], bhl.at[0, 24:27], -1, r_up)
    hl_next_end = remote(HL_NEXT, rn.at[8:11], bhl.at[0, 40:43], -2, r_up)
    hr_prev_in = remote(HR_PREV, ln.at[21:24], bhr.at[0, 21:24], 1, r_dn)
    hr_prev_end = remote(HR_PREV, ln.at[21:24], bhr.at[0, 5:8], 2, r_dn)
    az_prev = remote(AZ_PREV, az.at[24:40], az.at[8:24], 1, r)
    az_next = remote(AZ_NEXT, az.at[24:40], az.at[40:56], -1, r)
    y_prev = remote(Y_PREV, w.at[:, :, 18:24], w.at[:, :, 2:8], 1, r)
    y_next = remote(Y_NEXT, w.at[:, :, 8:14], w.at[:, :, 24:30], -1, r)
    swap = remote(SWAP, sp, sq, n_az // 2, r)

    hl_main.start()
    hr_main.start()

    @pl.when(last)
    def _():
        hl_full.start()
        hl_next_end.start()

    @pl.when(jnp.logical_not(last))
    def _():
        hl_next_in.start()

    @pl.when(first)
    def _():
        hr_full.start()
        hr_prev_end.start()

    @pl.when(jnp.logical_not(first))
    def _():
        hr_prev_in.start()

    hl_prev.start()
    hr_next.start()

    @pl.when(edge)
    def _():
        az_prev.start()
        az_next.start()

    y_prev.start()
    y_next.start()

    zero = jnp.int32(0)
    s_raw = jnp.clip(off_ref[0], 0, 15)
    t_raw = jnp.clip(off_ref[1] - half_offset, 0, 15)
    s_f = jnp.where(first, s_raw, zero)
    s_l = jnp.where(last, s_raw, zero)
    t_f = jnp.where(first, t_raw, zero)
    t_l = jnp.where(last, t_raw, zero)
    end_l = jnp.where(last, 1, zero)
    end_f = jnp.where(first, 1, zero)

    hl_main.wait_recv()
    hr_main.wait_recv()
    hl_prev.wait_recv()
    hr_next.wait_recv()
    hl_next_in.wait_recv()
    hr_prev_in.wait_recv()

    @pl.when(first)
    def _():
        hl_full.wait_recv()

    @pl.when(last)
    def _():
        hr_full.wait_recv()

    @pl.when(edge)
    def _():
        az_prev.wait_recv()
        az_next.wait_recv()

    def jump(fields, mask_l, mask_r):
        add = jnp.where(mask_l, shear_speed, 0.0) - jnp.where(mask_r, shear_speed, 0.0)
        fields[2] = jnp.where(jnp.logical_or(mask_l, mask_r), fields[2] + add * fields[0], fields[2])

    win = 24
    hlf = bhl[1, pl.ds(5 + t_f, win), :]
    hln = bhl[0, pl.ds(5 + t_f, win), :]
    hrf = bhr[1, pl.ds(21 - t_l - end_l, win), :]
    hrn = bhr[0, pl.ds(21 - t_l - end_l, win), :]
    o_l = 21 + t_f - s_f
    ln2 = jnp.where(first, trail * az[pl.ds(o_l - end_f, win), :] + lead * az[pl.ds(o_l, win), :], own[0, 5:29, :])
    o_r = 21 - t_l - end_l + s_l
    rn2 = jnp.where(last, lead * az[pl.ds(o_r, win), :] + trail * az[pl.ds(o_r + 1, win), :], own[2, 5:29, :])
    e = [spread(f, hlf, hln, ln2, ln2, rn2, rn2, hrn, hrf) for f in range(8)]
    cols = lane % 32
    in_l = jnp.logical_and(cols >= 8, cols < 16)
    in_r = jnp.logical_and(cols >= 16, cols < 24)
    jump(e, jnp.logical_and(last, in_r), jnp.logical_and(first, in_l))
    inv, pres = aux(e)
    gx = flux(e, inv, pres, 0)
    gy = flux(e, inv, pres, 1)
    gz = flux(e, inv, pres, 2)
    for f in range(8):
        es[f, 0:24, :] = gy[f]
    for f in range(8):
        es[8 + f, 0:24, :] = e[f]
    strip = []
    for f in range(8):
        def y(k, f=f):
            return es[f, 3 + k:20 + k, :]
        def u(k, f=f):
            return es[8 + f, 3 + k:20 + k, :]
        ty = combine([y(1), y(2), y(3)], [y(-1), y(-2), y(-3)]) + VISC * (u(1) - 2.0 * u(0) + u(-1))
        es[16 + f, 0:24, :] = e[f] + lanes_along(gx[f], e[f]) + lane_layers_along(gz[f], e[f])
        es[16 + f, 3:20, :] = es[16 + f, 3:20, :] + ty
    at_l = jnp.logical_and(first, left_half)
    at_r = jnp.logical_and(last, jnp.logical_not(left_half))
    w_0 = jnp.where(left_half, lead, trail)
    w_1 = jnp.where(left_half, trail, lead)
    sheared = jnp.logical_or(at_l, at_r)
    for f in range(8):
        here, beyond = es[16 + f, 3:19, :], es[16 + f, 4:20, :]
        strip.append(jnp.where(sheared, w_0 * here + w_1 * beyond, here))
    jump(strip, at_l, at_r)
    packed = jnp.zeros((16, 128), jnp.float32)
    for f in range(8):
        src = jnp.where(first, strip[f], lane_roll(strip[f], -20))
        packed = jnp.where(slot_is[f], lane_roll(src, 4 * (f - 1)), packed)
    sp[...] = packed

    @pl.when(edge)
    def _():
        swap.start()

    for f in range(8):
        es[16 + f, 0:16, :] = strip[f]

    y_prev.wait_recv()
    y_next.wait_recv()
    low = pack(lambda f: w[f, :, 0:8, :], 8)
    high = pack(lambda f: w[f, :, 24:32, :], 8)
    for t in range(4):
        own[t, 0:8, :] = low[t]
        own[t, 24:32, :] = high[t]
    hln0, hln1 = bhl[0, pl.ds(5 + s_f, win), :], bhl[0, pl.ds(5 + s_f + end_f, win), :]
    hln = jnp.where(first, lead * hln0 + trail * hln1, hln0)
    o_r = 21 - s_l
    hrn0, hrn1 = bhr[0, pl.ds(o_r - end_l, win), :], bhr[0, pl.ds(o_r, win), :]
    hrn = jnp.where(last, trail * hrn0 + lead * hrn1, hrn1)
    mine = [own[t, 5:29, :] for t in range(4)]
    e = [spread(f, hln, hln, mine[0], mine[1], mine[3], mine[2], hrn, hrn) for f in range(8)]
    jump(e, jnp.logical_and(first, cols < 8), jnp.logical_and(last, cols >= 24))
    inv, pres = aux(e)
    gx = flux(e, inv, pres, 0)
    edge_x = [lanes_along(gx[f], e[f]) for f in range(8)]

    at_left, at_right = lane < 3, lane >= 125

    def mend(inner, strip_f):
        fixed = []
        for z in range(4):
            from_l = lane_roll(strip_f, -(32 * z + 8))
            from_r = lane_roll(strip_f, 104 - 32 * z)
            fixed.append(jnp.where(at_left, from_l, jnp.where(at_right, from_r, inner[z])))
        return jnp.stack(fixed)

    q = [w[f] for f in range(8)]
    inv, pres = aux(q)
    gy = flux(q, inv, pres, 1)
    for f in range(8):
        fy[f] = gy[f]
    q = [w[f, :, 5:29, :] for f in range(8)]
    inv, pres = aux(q)
    gx = flux(q, inv, pres, 0)
    gz = flux(q, inv, pres, 2)
    one = []
    for f in range(8):
        def y(k, f=f):
            return fy[f, :, 5 + k:29 + k, :]
        ty = combine([y(1), y(2), y(3)], [y(-1), y(-2), y(-3)])
        ty = ty + VISC * (w[f, :, 6:30, :] - 2.0 * q[f] + w[f, :, 4:28, :])
        one.append(q[f] + mend(lanes_along(gx[f], q[f]), edge_x[f]) + ty + layers_along(gz[f], q[f]))
    inv, pres = aux(one)
    gy = flux(one, inv, pres, 1)
    start = [0.5 * w[f, :, 8:24, :] for f in range(8)]

    @pl.when(edge)
    def _():
        swap.wait_send()

    for k, c in enumerate((hl_main, hr_main, hl_prev, hr_next, hl_next_in, hr_prev_in, y_prev, y_next)):
        c.wait_send()

    @pl.when(last)
    def _():
        hl_full.wait_send()

    @pl.when(first)
    def _():
        hr_full.wait_send()

    @pl.when(edge)
    def _():
        az_prev.wait_send()
        az_next.wait_send()

    for f in range(8):
        w[f, :, 0:24, :] = one[f]
        fy[f, :, 0:24, :] = gy[f]

    q = [w[f, :, 3:19, :] for f in range(8)]
    inv, pres = aux(q)
    gx = flux(q, inv, pres, 0)
    gz = flux(q, inv, pres, 2)
    tiles = pack(lambda f: q[f], 16)
    for f in range(8):
        def y(k, f=f):
            return fy[f, :, 3 + k:19 + k, :]
        ty = combine([y(1), y(2), y(3)], [y(-1), y(-2), y(-3)])
        ty = ty + VISC * (w[f, :, 4:20, :] - 2.0 * q[f] + w[f, :, 2:18, :])
        out[f] = start[f] + 0.5 * (q[f] + ty + layers_along(gz[f], q[f]))
    inner = [lanes_along(gx[f], q[f]) for f in range(8)]

    @pl.when(edge)
    def _():
        swap.wait_recv()

    got = sq[...]
    near_l = jnp.logical_and(first, cols < 8)
    near_r = jnp.logical_and(last, cols >= 24)
    own_cols = jnp.logical_and(cols >= 8, cols < 24)
    e = []
    for f in range(8):
        ghost = es[16 + f, 0:16, :]
        ghost = jnp.where(near_l, lane_roll(got, 4 * (1 - f)), ghost)
        ghost = jnp.where(near_r, lane_roll(got, 4 * (6 - f)), ghost)
        mid = spread(f, tiles[0], tiles[0], tiles[0], tiles[1], tiles[3], tiles[2], tiles[2], tiles[2])
        e.append(jnp.where(own_cols, mid, ghost))
    inv, pres = aux(e)
    gx = flux(e, inv, pres, 0)
    for f in range(8):
        out[f] = out[f] + 0.5 * mend(inner[f], lanes_along(gx[f], e[f]))


def solution(mesh):
    n_az, n_rad = mesh.shape["az"], mesh.shape["rad"]

    def shards(density, momentum, magnetic, tracer, shear_offset):
        half = n_az // 2 * density.shape[1]
        f32 = jnp.float32
        anywhere = pl.BlockSpec(memory_space=pl.ANY)
        return pl.pallas_call(
            functools.partial(kernel, n_az, n_rad, half),
            out_shape=jax.ShapeDtypeStruct((8, 4, 16, 128), f32),
            in_specs=[pl.BlockSpec(memory_space=pltpu.SMEM)] + [anywhere] * 4,
            out_specs=pl.BlockSpec(memory_space=pltpu.VMEM),
            scratch_shapes=[
                pltpu.VMEM((8, 4, 32, 128), f32),
                pltpu.VMEM((8, 4, 32, 128), f32),
                pltpu.VMEM((4, 32, 128), f32),
                pltpu.VMEM((2, 48, 128), f32),
                pltpu.VMEM((2, 48, 128), f32),
                pltpu.VMEM((64, 128), f32),
                pltpu.VMEM((24, 32, 128), f32),
                pltpu.VMEM((16, 128), f32),
                pltpu.VMEM((16, 128), f32),
                pltpu.SemaphoreType.DMA((4,)),
                pltpu.SemaphoreType.DMA((N_COPY,)),
                pltpu.SemaphoreType.DMA((N_COPY,)),
            ],
            compiler_params=pltpu.CompilerParams(collective_id=0, has_side_effects=True),
        )(shear_offset, density, momentum, magnetic, tracer)

    placed = (
        P(None, "az", "rad"),
        P(None, None, "az", "rad"),
        P(None, None, "az", "rad"),
        P(None, "az", "rad"),
        P(),
    )
    return jax.shard_map(
        shards, mesh=mesh, in_specs=placed, out_specs=P(None, None, "az", "rad"), check_vma=False
    )
```

```python
import functools

import jax
import jax.numpy as jnp
from jax import lax
from jax.experimental import pallas as pl
from jax.experimental.pallas import tpu as pltpu
from jax.sharding import PartitionSpec as P

time_step = 0.025
viscosity = 0.5
sound_squared = 1.0
shear_speed = 1.0
frac_weight = 0.375

MESH = pl.DeviceIdType.MESH
D1 = -time_step * 45.0 / 60.0
D2 = time_step * 9.0 / 60.0
D3 = -time_step / 60.0
VISC = time_step * viscosity
lead = 1.0 - frac_weight
trail = frac_weight

Y_PREV, Y_NEXT, HL_MAIN, HL_PREV, HL_NEXT, HL_FULL, HR_MAIN, HR_NEXT, HR_PREV, HR_FULL, AZ_PREV, AZ_NEXT, SWAP = range(13)
N_COPY = 13


def flux(q, inv, pres, d):
    vel = [q[1 + i] * inv for i in range(3)]
    mag = q[4:7]
    vd, bd = vel[d], mag[d]
    out = [q[1 + d]]
    for i in range(3):
        g = q[1 + i] * vd - mag[i] * bd
        out.append(g + pres if i == d else g)
    for i in range(3):
        out.append(vd * mag[i] - bd * vel[i])
    out.append(q[7] * vd)
    return out


def aux(q):
    inv = 1.0 / q[0]
    pres = sound_squared * q[0] + 0.5 * (q[4] * q[4] + q[5] * q[5] + q[6] * q[6])
    return inv, pres


def combine(up, down):
    return D1 * (up[0] - down[0]) + D2 * (up[1] - down[1]) + D3 * (up[2] - down[2])


def lane_roll(x, shift):
    shift %= 128
    return x if shift == 0 else pltpu.roll(x, shift, x.ndim - 1)


def lanes_along(g, u):
    r = combine([lane_roll(g, -k) for k in (1, 2, 3)], [lane_roll(g, k) for k in (1, 2, 3)])
    return r + VISC * (lane_roll(u, -1) - 2.0 * u + lane_roll(u, 1))


def around(x, k):
    k %= x.shape[0]
    return x if k == 0 else jnp.concatenate([x[k:], x[:k]], axis=0)


def layers_along(g, u):
    r = combine([around(g, k) for k in (1, 2, 3)], [around(g, -k) for k in (1, 2, 3)])
    return r + VISC * (around(u, 1) - 2.0 * u + around(u, -1))


def lane_layers_along(g, u):
    r = combine([lane_roll(g, -32 * k) for k in (1, 2, 3)], [lane_roll(g, 32 * k) for k in (1, 2, 3)])
    return r + VISC * (lane_roll(u, -32) - 2.0 * u + lane_roll(u, 32))


def kernel(n_az, n_rad, run, half_offset, off_hbm, den, mom, mag, tra, out,
           off_ref, w, s1, fy, own, bhl, bhr, az, es, sp, sq, in_sem, send, recv):
    a = lax.axis_index("az")
    r = lax.axis_index("rad")
    first = r == 0
    last = r == n_rad - 1
    edge = jnp.logical_or(first, last)
    r_up = lax.rem(r + 1, n_rad)
    r_dn = lax.rem(r + n_rad - 1, n_rad)

    def at(step):
        return lax.rem(a + step + n_az, n_az)

    def dev(step, to_r):
        return (at(step), to_r)

    barrier = pltpu.get_barrier_semaphore()

    def greet(step, to_r):
        pl.semaphore_signal(barrier, inc=1, device_id=dev(step, to_r), device_id_type=MESH)

    even = lax.rem(r, 2) == 0
    odd = jnp.logical_not(even)
    place = lax.rem(a, run)
    head, tail = place == 0, place == run - 1
    odd_head, odd_tail = jnp.logical_and(odd, head), jnp.logical_and(odd, tail)

    @pl.when(even)
    def _():
        for step in (-1, 0, 1):
            greet(step, r_up)
            greet(step, r_dn)

    @pl.when(first)
    def _():
        greet(2, r_dn)

    @pl.when(edge)
    def _():
        greet(n_az // 2, r)

    @pl.when(jnp.logical_or(even, jnp.logical_not(tail)))
    def _():
        greet(1, r)

    @pl.when(jnp.logical_or(even, head))
    def _():
        greet(-1, r)

    rows = pl.ds(8, 16)
    loads = [
        pltpu.make_async_copy(den, w.at[0, :, rows], in_sem.at[0]),
        pltpu.make_async_copy(mom, w.at[1:4, :, rows], in_sem.at[1]),
        pltpu.make_async_copy(mag, w.at[4:7, :, rows], in_sem.at[2]),
        pltpu.make_async_copy(tra, w.at[7, :, rows], in_sem.at[3]),
    ]
    offsets = pltpu.make_async_copy(off_hbm, off_ref, in_sem.at[4])
    for c in loads:
        c.start()
    offsets.start()
    w[:, :, 0:2, :] = jnp.ones((8, 4, 2, 128), jnp.float32)
    w[:, :, 30:32, :] = jnp.ones((8, 4, 2, 128), jnp.float32)
    for c in loads:
        c.wait()

    lane = lax.broadcasted_iota(jnp.int32, (1, 128), 1)
    group = lane // 4
    slot_is = [lane % 32 // 4 == k for k in range(8)]
    left_half = lane % 32 < 16

    def pack(read, count):
        tiles = [jnp.zeros((count, 128), jnp.float32)] * 4
        for f in range(8):
            x = read(f)
            for z in range(4):
                moved = lane_roll(x[z], 32 * z + 4 * f)
                for t, shift in enumerate((0, 1, -1, -2)):
                    here = group == (8 * z + f + shift) % 32
                    tiles[t] = jnp.where(here, moved, tiles[t])
        return tiles

    def spread(f, hlf, hln, ln, lf, rf, rn, hrn, hrf):
        def of(k):
            return slot_is[(f + k) % 8]
        left = jnp.where(of(-2), hlf, jnp.where(of(-1), hln, jnp.where(of(0), ln, lf)))
        right = jnp.where(of(-2), rf, jnp.where(of(-1), rn, jnp.where(of(0), hrn, hrf)))
        return jnp.where(left_half, lane_roll(left, 4 * (2 - f)), lane_roll(right, 4 * (6 - f)))

    tiles = pack(lambda f: w[f, :, 8:24, :], 16)
    for t in range(4):
        own[t, 8:24, :] = tiles[t]
    az[24:40, :] = jnp.where(first, tiles[0], tiles[2])

    one = jnp.int32(1)
    zero = jnp.int32(0)
    along = jnp.where(even, 2 * one, jnp.where(head, zero, jnp.where(tail, 2 * one, one)))
    across = jnp.where(even, zero, jnp.where(last, 7 * one, 6 * one))
    pl.semaphore_wait(barrier, along + across + jnp.where(edge, one, zero))

    def remote(k, src, dst, step, to_r):
        return pltpu.make_async_remote_copy(
            src_ref=src, dst_ref=dst, send_sem=send.at[k], recv_sem=recv.at[k],
            device_id=dev(step, to_r), device_id_type=MESH)

    own_l, own_r = own.at[0:2, 8:24], own.at[2:4, 8:24]
    ln, rn = own.at[0], own.at[2]
    hl_main = remote(HL_MAIN, own_r, bhl.at[:, 8:24], 0, r_up)
    hr_main = remote(HR_MAIN, own_l, bhr.at[:, 24:40], 0, r_dn)
    hl_full = remote(HL_FULL, own_r, bhl.at[:, 24:40], -1, r_up)
    hr_full = remote(HR_FULL, own_l, bhr.at[:, 8:24], 1, r_dn)
    hl_prev = remote(HL_PREV, rn.at[21:24], bhl.at[0, 5:8], 1, r_up)
    hr_next = remote(HR_NEXT, ln.at[8:11], bhr.at[0, 40:43], -1, r_dn)
    hl_next_in = remote(HL_NEXT, rn.at[8:11], bhl.at[0, 24:27], -1, r_up)
    hl_next_end = remote(HL_NEXT, rn.at[8:11], bhl.at[0, 40:43], -2, r_up)
    hr_prev_in = remote(HR_PREV, ln.at[21:24], bhr.at[0, 21:24], 1, r_dn)
    hr_prev_end = remote(HR_PREV, ln.at[21:24], bhr.at[0, 5:8], 2, r_dn)
    az_prev = remote(AZ_PREV, az.at[24:40], az.at[8:24], 1, r)
    az_next = remote(AZ_NEXT, az.at[24:40], az.at[40:56], -1, r)
    y_prev = remote(Y_PREV, w.at[:, :, 18:24], w.at[:, :, 2:8], 1, r)
    y_next = remote(Y_NEXT, w.at[:, :, 8:14], w.at[:, :, 24:30], -1, r)
    swap = remote(SWAP, sp, sq, n_az // 2, r)

    def send_strips():
        hl_main.start()
        hr_main.start()

        @pl.when(last)
        def _():
            hl_full.start()
            hl_next_end.start()

        @pl.when(jnp.logical_not(last))
        def _():
            hl_next_in.start()

        @pl.when(first)
        def _():
            hr_full.start()
            hr_prev_end.start()

        @pl.when(jnp.logical_not(first))
        def _():
            hr_prev_in.start()

        hl_prev.start()
        hr_next.start()

    def send_up():
        @pl.when(edge)
        def _():
            az_prev.start()
        y_prev.start()

    def send_down():
        @pl.when(edge)
        def _():
            az_next.start()
        y_next.start()

    pl.when(odd)(send_strips)
    pl.when(jnp.logical_or(even, tail))(send_up)
    pl.when(jnp.logical_not(odd_head))(send_down)

    @pl.when(jnp.logical_and(odd, jnp.logical_not(tail)))
    def _():
        y_next.wait_recv()
        send_up()

    @pl.when(odd_head)
    def _():
        y_prev.wait_recv()
        send_down()

    @pl.when(jnp.logical_or(even, tail))
    def _():
        y_next.wait_recv()

    @pl.when(jnp.logical_not(odd_head))
    def _():
        y_prev.wait_recv()

    cols = lane % 32

    edge_lane = jnp.logical_or(lane < 3, lane >= 125)

    def edges(strip_f):
        joined = jnp.where(jnp.logical_and(cols >= 5, cols < 8), lane_roll(strip_f, -16), strip_f)
        return jnp.stack([jnp.where(edge_lane, lane_roll(joined, -(32 * z + 8)), 0.0) for z in range(4)])

    low = pack(lambda f: w[f, :, 0:8, :], 8)
    high = pack(lambda f: w[f, :, 24:32, :], 8)
    for t in range(4):
        own[t, 0:8, :] = low[t]
        own[t, 24:32, :] = high[t]
    q = [w[f] for f in range(8)]
    inv, pres = aux(q)
    gy = flux(q, inv, pres, 1)
    for f in range(8):
        fy[f] = gy[f]
    q = [w[f, :, 5:29, :] for f in range(8)]
    inv, pres = aux(q)
    gx = flux(q, inv, pres, 0)
    gz = flux(q, inv, pres, 2)
    for f in range(8):
        def y(k, f=f):
            return fy[f, :, 5 + k:29 + k, :]
        ty = combine([y(1), y(2), y(3)], [y(-1), y(-2), y(-3)])
        ty = ty + VISC * (w[f, :, 6:30, :] - 2.0 * q[f] + w[f, :, 4:28, :])
        tx = jnp.where(edge_lane, 0.0, lanes_along(gx[f], q[f]))
        s1[f, :, 0:24, :] = q[f] + tx + ty + layers_along(gz[f], q[f])

    offsets.wait()
    s_raw = jnp.clip(off_ref[0], 0, 15)
    t_raw = jnp.clip(off_ref[1] - half_offset, 0, 15)
    s_f = jnp.where(first, s_raw, zero)
    s_l = jnp.where(last, s_raw, zero)
    t_f = jnp.where(first, t_raw, zero)
    t_l = jnp.where(last, t_raw, zero)
    end_l = jnp.where(last, 1, zero)
    end_f = jnp.where(first, 1, zero)

    hl_main.wait_recv()
    hr_main.wait_recv()
    hl_prev.wait_recv()
    hr_next.wait_recv()
    hl_next_in.wait_recv()
    hr_prev_in.wait_recv()

    @pl.when(first)
    def _():
        hl_full.wait_recv()

    @pl.when(last)
    def _():
        hr_full.wait_recv()

    @pl.when(edge)
    def _():
        az_prev.wait_recv()
        az_next.wait_recv()

    def jump(fields, mask_l, mask_r):
        add = jnp.where(mask_l, shear_speed, 0.0) - jnp.where(mask_r, shear_speed, 0.0)
        fields[2] = jnp.where(jnp.logical_or(mask_l, mask_r), fields[2] + add * fields[0], fields[2])

    win = 24
    hlf = bhl[1, pl.ds(5 + t_f, win), :]
    hln = bhl[0, pl.ds(5 + t_f, win), :]
    hrf = bhr[1, pl.ds(21 - t_l - end_l, win), :]
    hrn = bhr[0, pl.ds(21 - t_l - end_l, win), :]
    o_l = 21 + t_f - s_f
    ln2 = jnp.where(first, trail * az[pl.ds(o_l - end_f, win), :] + lead * az[pl.ds(o_l, win), :], own[0, 5:29, :])
    o_r = 21 - t_l - end_l + s_l
    rn2 = jnp.where(last, lead * az[pl.ds(o_r, win), :] + trail * az[pl.ds(o_r + 1, win), :], own[2, 5:29, :])
    e = [spread(f, hlf, hln, ln2, ln2, rn2, rn2, hrn, hrf) for f in range(8)]
    in_l = jnp.logical_and(cols >= 8, cols < 16)
    in_r = jnp.logical_and(cols >= 16, cols < 24)
    jump(e, jnp.logical_and(last, in_r), jnp.logical_and(first, in_l))
    inv, pres = aux(e)
    gx = flux(e, inv, pres, 0)
    gy = flux(e, inv, pres, 1)
    gz = flux(e, inv, pres, 2)
    for f in range(8):
        es[f, 0:24, :] = gy[f]
    for f in range(8):
        es[8 + f, 0:24, :] = e[f]
    strip = []
    for f in range(8):
        def y(k, f=f):
            return es[f, 3 + k:20 + k, :]
        def u(k, f=f):
            return es[8 + f, 3 + k:20 + k, :]
        ty = combine([y(1), y(2), y(3)], [y(-1), y(-2), y(-3)]) + VISC * (u(1) - 2.0 * u(0) + u(-1))
        es[16 + f, 0:24, :] = e[f] + lanes_along(gx[f], e[f]) + lane_layers_along(gz[f], e[f])
        es[16 + f, 3:20, :] = es[16 + f, 3:20, :] + ty
    at_l = jnp.logical_and(first, left_half)
    at_r = jnp.logical_and(last, jnp.logical_not(left_half))
    w_0 = jnp.where(left_half, lead, trail)
    w_1 = jnp.where(left_half, trail, lead)
    sheared = jnp.logical_or(at_l, at_r)
    for f in range(8):
        here, beyond = es[16 + f, 3:19, :], es[16 + f, 4:20, :]
        strip.append(jnp.where(sheared, w_0 * here + w_1 * beyond, here))
    jump(strip, at_l, at_r)
    packed = jnp.zeros((16, 128), jnp.float32)
    for f in range(8):
        src = jnp.where(first, strip[f], lane_roll(strip[f], -20))
        packed = jnp.where(slot_is[f], lane_roll(src, 4 * (f - 1)), packed)
    sp[...] = packed

    @pl.when(edge)
    def _():
        swap.start()

    pl.when(even)(send_strips)

    for f in range(8):
        es[16 + f, 0:16, :] = strip[f]

    hln0, hln1 = bhl[0, pl.ds(5 + s_f, win), :], bhl[0, pl.ds(5 + s_f + end_f, win), :]
    hln = jnp.where(first, lead * hln0 + trail * hln1, hln0)
    o_r = 21 - s_l
    hrn0, hrn1 = bhr[0, pl.ds(o_r - end_l, win), :], bhr[0, pl.ds(o_r, win), :]
    hrn = jnp.where(last, trail * hrn0 + lead * hrn1, hrn1)
    mine = [own[t, 5:29, :] for t in range(4)]
    e = [spread(f, hln, hln, mine[0], mine[1], mine[3], mine[2], hrn, hrn) for f in range(8)]
    jump(e, jnp.logical_and(first, cols < 8), jnp.logical_and(last, cols >= 24))
    inv, pres = aux(e)
    gx = flux(e, inv, pres, 0)
    for f in range(8):
        s1[f, :, 0:24, :] = s1[f, :, 0:24, :] + edges(lanes_along(gx[f], e[f]))

    q = [s1[f, :, 0:24, :] for f in range(8)]
    inv, pres = aux(q)
    gy = flux(q, inv, pres, 1)
    for f in range(8):
        fy[f, :, 0:24, :] = gy[f]
    q = [s1[f, :, 3:19, :] for f in range(8)]
    inv, pres = aux(q)
    gx = flux(q, inv, pres, 0)
    gz = flux(q, inv, pres, 2)
    tiles = pack(lambda f: q[f], 16)
    for f in range(8):
        def y(k, f=f):
            return fy[f, :, 3 + k:19 + k, :]
        ty = combine([y(1), y(2), y(3)], [y(-1), y(-2), y(-3)])
        ty = ty + VISC * (s1[f, :, 4:20, :] - 2.0 * q[f] + s1[f, :, 2:18, :])
        tx = jnp.where(edge_lane, 0.0, lanes_along(gx[f], q[f]))
        out[f] = 0.5 * w[f, :, 8:24, :] + 0.5 * (q[f] + tx + ty + layers_along(gz[f], q[f]))
    own_cols = jnp.logical_and(cols >= 8, cols < 24)
    for f in range(8):
        mid = spread(f, tiles[0], tiles[0], tiles[0], tiles[1], tiles[3], tiles[2], tiles[2], tiles[2])
        es[16 + f, 0:16, :] = jnp.where(own_cols, mid, es[16 + f, 0:16, :])

    @pl.when(edge)
    def _():
        swap.wait_recv()

    got = sq[...]
    got = jnp.where(last, lane_roll(got, 20), got)
    theirs = jnp.logical_or(jnp.logical_and(first, cols < 8), jnp.logical_and(last, cols >= 24))
    e = [jnp.where(theirs, lane_roll(got, 4 * (1 - f)), es[16 + f, 0:16, :]) for f in range(8)]
    inv, pres = aux(e)
    gx = flux(e, inv, pres, 0)
    for f in range(8):
        out[f] = out[f] + edges(0.5 * lanes_along(gx[f], e[f]))

    @pl.when(edge)
    def _():
        swap.wait_send()

    for c in (hl_main, hr_main, hl_prev, hr_next, hl_next_in, hr_prev_in, y_prev, y_next):
        c.wait_send()

    @pl.when(last)
    def _():
        hl_full.wait_send()

    @pl.when(first)
    def _():
        hr_full.wait_send()

    @pl.when(edge)
    def _():
        az_prev.wait_send()
        az_next.wait_send()


def solution(mesh):
    n_az, n_rad = mesh.shape["az"], mesh.shape["rad"]

    def shards(density, momentum, magnetic, tracer, shear_offset):
        half = n_az // 2 * density.shape[1]
        f32 = jnp.float32
        anywhere = pl.BlockSpec(memory_space=pl.ANY)
        return pl.pallas_call(
            functools.partial(kernel, n_az, n_rad, 12 if n_az % 12 == 0 else 2, half),
            out_shape=pltpu.VMEM((8, 4, 16, 128), f32),
            in_specs=[anywhere] * 5,
            out_specs=pl.BlockSpec(memory_space=pltpu.VMEM),
            scratch_shapes=[
                pltpu.SMEM((2,), jnp.int32),
                pltpu.VMEM((8, 4, 32, 128), f32),
                pltpu.VMEM((8, 4, 32, 128), f32),
                pltpu.VMEM((8, 4, 32, 128), f32),
                pltpu.VMEM((4, 32, 128), f32),
                pltpu.VMEM((2, 48, 128), f32),
                pltpu.VMEM((2, 48, 128), f32),
                pltpu.VMEM((64, 128), f32),
                pltpu.VMEM((24, 32, 128), f32),
                pltpu.VMEM((16, 128), f32),
                pltpu.VMEM((16, 128), f32),
                pltpu.SemaphoreType.DMA((5,)),
                pltpu.SemaphoreType.DMA((N_COPY,)),
                pltpu.SemaphoreType.DMA((N_COPY,)),
            ],
            compiler_params=pltpu.CompilerParams(collective_id=0, has_side_effects=True),
        )(shear_offset, density, momentum, magnetic, tracer)

    placed = (
        P(None, "az", "rad"),
        P(None, None, "az", "rad"),
        P(None, None, "az", "rad"),
        P(None, "az", "rad"),
        P(),
    )
    return jax.shard_map(
        shards, mesh=mesh, in_specs=placed, out_specs=P(None, None, "az", "rad"), check_vma=False
    )
```

```python
import functools

import jax
import jax.numpy as jnp
from jax import lax
from jax.experimental import pallas as pl
from jax.experimental.pallas import tpu as pltpu
from jax.sharding import PartitionSpec as P

time_step = 0.025
viscosity = 0.5
sound_squared = 1.0
shear_speed = 1.0
frac_weight = 0.375

MESH = pl.DeviceIdType.MESH
D1 = -time_step * 45.0 / 60.0
D2 = time_step * 9.0 / 60.0
D3 = -time_step / 60.0
VISC = time_step * viscosity
lead = 1.0 - frac_weight
trail = frac_weight

S_MAIN, S_CORNER, S_FULL, S_AZ, S_Y, S_SWAP = range(6)
R_LEFT, R_RIGHT, R_FULL, R_AZ, R_PREV, R_NEXT, R_SWAP = range(7)


def flux(q, inv, pres, d):
    vel = [q[1 + i] * inv for i in range(3)]
    mag = q[4:7]
    vd, bd = vel[d], mag[d]
    out = [q[1 + d]]
    for i in range(3):
        g = q[1 + i] * vd - mag[i] * bd
        out.append(g + pres if i == d else g)
    for i in range(3):
        out.append(vd * mag[i] - bd * vel[i])
    out.append(q[7] * vd)
    return out


def aux(q):
    inv = 1.0 / q[0]
    pres = sound_squared * q[0] + 0.5 * (q[4] * q[4] + q[5] * q[5] + q[6] * q[6])
    return inv, pres


def combine(up, down):
    return D1 * (up[0] - down[0]) + D2 * (up[1] - down[1]) + D3 * (up[2] - down[2])


def lane_roll(x, shift):
    shift %= 128
    return x if shift == 0 else pltpu.roll(x, shift, x.ndim - 1)


def lanes_along(g, u):
    r = combine([lane_roll(g, -k) for k in (1, 2, 3)], [lane_roll(g, k) for k in (1, 2, 3)])
    return r + VISC * (lane_roll(u, -1) - 2.0 * u + lane_roll(u, 1))


def around(x, k):
    k %= x.shape[0]
    return x if k == 0 else jnp.concatenate([x[k:], x[:k]], axis=0)


def layers_along(g, u):
    r = combine([around(g, k) for k in (1, 2, 3)], [around(g, -k) for k in (1, 2, 3)])
    return r + VISC * (around(u, 1) - 2.0 * u + around(u, -1))


def lane_layers_along(g, u):
    r = combine([lane_roll(g, -32 * k) for k in (1, 2, 3)], [lane_roll(g, 32 * k) for k in (1, 2, 3)])
    return r + VISC * (lane_roll(u, -32) - 2.0 * u + lane_roll(u, 32))


def kernel(n_az, n_rad, run, half_offset, off_hbm, den, mom, mag, tra, out,
           off_ref, w, s1, fy, own, bhl, bhr, az, es, sp, sq, in_sem, send, recv, go):
    a = lax.axis_index("az")
    r = lax.axis_index("rad")
    first = r == 0
    last = r == n_rad - 1
    edge = jnp.logical_or(first, last)
    r_up = lax.rem(r + 1, n_rad)
    r_dn = lax.rem(r + n_rad - 1, n_rad)

    def at(step):
        return lax.rem(a + step + n_az, n_az)

    def dev(step, to_r):
        return (at(step), to_r)

    rows = pl.ds(8, 16)
    loads = [
        pltpu.make_async_copy(den, w.at[0, :, rows], in_sem.at[0]),
        pltpu.make_async_copy(mom, w.at[1:4, :, rows], in_sem.at[0]),
        pltpu.make_async_copy(mag, w.at[4:7, :, rows], in_sem.at[0]),
        pltpu.make_async_copy(tra, w.at[7, :, rows], in_sem.at[0]),
    ]
    offsets = pltpu.make_async_copy(off_hbm, off_ref, in_sem.at[1])
    for c in loads:
        c.start()
    offsets.start()

    barrier = pltpu.get_barrier_semaphore()

    def greet(step, to_r):
        pl.semaphore_signal(barrier, inc=1, device_id=dev(step, to_r), device_id_type=MESH)

    even = lax.rem(r, 2) == 0
    odd = jnp.logical_not(even)
    place = lax.rem(a, run)
    head, tail = place == 0, place == run - 1
    odd_head, odd_tail = jnp.logical_and(odd, head), jnp.logical_and(odd, tail)

    @pl.when(even)
    def _():
        for step in (-1, 0, 1):
            greet(step, r_up)
            greet(step, r_dn)

    @pl.when(first)
    def _():
        greet(2, r_dn)

    greets_half = jnp.logical_or(first, jnp.logical_and(last, head))
    told = jnp.logical_and(last, jnp.logical_not(head))

    @pl.when(greets_half)
    def _():
        greet(n_az // 2, r)

    @pl.when(jnp.logical_or(even, jnp.logical_not(tail)))
    def _():
        greet(1, r)

    @pl.when(jnp.logical_or(even, head))
    def _():
        greet(-1, r)

    w[:, :, 0:2, :] = jnp.ones((8, 4, 2, 128), jnp.float32)
    w[:, :, 30:32, :] = jnp.ones((8, 4, 2, 128), jnp.float32)
    block = w.at[:, :, rows]
    pltpu.make_async_copy(block, block, in_sem.at[0]).wait()

    lane = lax.broadcasted_iota(jnp.int32, (1, 128), 1)
    group = lane // 4
    slot_is = [lane % 32 // 4 == k for k in range(8)]
    left_half = lane % 32 < 16

    def pack(read, count):
        tiles = [jnp.zeros((count, 128), jnp.float32)] * 4
        for f in range(8):
            x = read(f)
            for z in range(4):
                moved = lane_roll(x[z], 32 * z + 4 * f)
                for t, shift in enumerate((0, 1, -1, -2)):
                    here = group == (8 * z + f + shift) % 32
                    tiles[t] = jnp.where(here, moved, tiles[t])
        return tiles

    def spread(f, hlf, hln, ln, lf, rf, rn, hrn, hrf):
        def of(k):
            return slot_is[(f + k) % 8]
        left = jnp.where(of(-2), hlf, jnp.where(of(-1), hln, jnp.where(of(0), ln, lf)))
        right = jnp.where(of(-2), rf, jnp.where(of(-1), rn, jnp.where(of(0), hrn, hrf)))
        return jnp.where(left_half, lane_roll(left, 4 * (2 - f)), lane_roll(right, 4 * (6 - f)))

    tiles = pack(lambda f: w[f, :, 8:24, :], 16)
    for t in range(4):
        own[t, 8:24, :] = tiles[t]
    az[24:40, :] = jnp.where(first, tiles[0], tiles[2])

    one = jnp.int32(1)
    zero = jnp.int32(0)
    along = jnp.where(even, 2 * one, jnp.where(head, zero, jnp.where(tail, 2 * one, one)))
    across = jnp.where(even, zero, jnp.where(last, 7 * one, 6 * one))
    pl.semaphore_wait(barrier, along + across + jnp.where(greets_half, one, zero))

    def remote(k, n, src, dst, step, to_r):
        return pltpu.make_async_remote_copy(
            src_ref=src, dst_ref=dst, send_sem=send.at[k], recv_sem=recv.at[n],
            device_id=dev(step, to_r), device_id_type=MESH)

    def arrived(ref, sem):
        pltpu.make_async_copy(ref, ref, sem).wait()

    own_l, own_r = own.at[0:2, 8:24], own.at[2:4, 8:24]
    ln, rn = own.at[0], own.at[2]
    hl_main = remote(S_MAIN, R_LEFT, own_r, bhl.at[:, 8:24], 0, r_up)
    hr_main = remote(S_MAIN, R_RIGHT, own_l, bhr.at[:, 24:40], 0, r_dn)
    hl_full = remote(S_FULL, R_FULL, own_r, bhl.at[:, 24:40], -1, r_up)
    hr_full = remote(S_FULL, R_FULL, own_l, bhr.at[:, 8:24], 1, r_dn)
    hl_prev = remote(S_CORNER, R_LEFT, rn.at[21:24], bhl.at[0, 5:8], 1, r_up)
    hr_next = remote(S_CORNER, R_RIGHT, ln.at[8:11], bhr.at[0, 40:43], -1, r_dn)
    hl_next_in = remote(S_CORNER, R_LEFT, rn.at[8:11], bhl.at[0, 24:27], -1, r_up)
    hl_next_end = remote(S_CORNER, R_LEFT, rn.at[8:11], bhl.at[0, 40:43], -2, r_up)
    hr_prev_in = remote(S_CORNER, R_RIGHT, ln.at[21:24], bhr.at[0, 21:24], 1, r_dn)
    hr_prev_end = remote(S_CORNER, R_RIGHT, ln.at[21:24], bhr.at[0, 5:8], 2, r_dn)
    az_prev = remote(S_AZ, R_AZ, az.at[24:40], az.at[8:24], 1, r)
    az_next = remote(S_AZ, R_AZ, az.at[24:40], az.at[40:56], -1, r)
    y_prev = remote(S_Y, R_PREV, w.at[:, :, 18:24], w.at[:, :, 2:8], 1, r)
    y_next = remote(S_Y, R_NEXT, w.at[:, :, 8:14], w.at[:, :, 24:30], -1, r)
    swap = remote(S_SWAP, R_SWAP, sp, sq, n_az // 2, r)

    def send_right():
        hl_main.start()

        @pl.when(last)
        def _():
            hl_full.start()
            hl_next_end.start()

        @pl.when(jnp.logical_not(last))
        def _():
            hl_next_in.start()

        hl_prev.start()

    def send_left():
        hr_main.start()

        @pl.when(first)
        def _():
            hr_full.start()
            hr_prev_end.start()

        @pl.when(jnp.logical_not(first))
        def _():
            hr_prev_in.start()

        hr_next.start()

    def send_up():
        @pl.when(edge)
        def _():
            az_prev.start()
        y_prev.start()

    def send_down():
        @pl.when(edge)
        def _():
            az_next.start()
        y_next.start()

    pl.when(odd)(send_right)
    pl.when(odd)(send_left)
    pl.when(jnp.logical_or(even, tail))(send_up)
    pl.when(jnp.logical_not(odd_head))(send_down)

    @pl.when(jnp.logical_and(odd, jnp.logical_not(tail)))
    def _():
        y_next.wait_recv()
        send_up()

    @pl.when(odd_head)
    def _():
        y_prev.wait_recv()
        send_down()

    @pl.when(jnp.logical_or(even, tail))
    def _():
        y_next.wait_recv()

    @pl.when(jnp.logical_not(odd_head))
    def _():
        y_prev.wait_recv()

    cols = lane % 32

    edge_lane = jnp.logical_or(lane < 3, lane >= 125)

    def edges(strip_f):
        joined = jnp.where(jnp.logical_and(cols >= 5, cols < 8), lane_roll(strip_f, -16), strip_f)
        return jnp.stack([jnp.where(edge_lane, lane_roll(joined, -(32 * z + 8)), 0.0) for z in range(4)])

    low = pack(lambda f: w[f, :, 0:8, :], 8)
    high = pack(lambda f: w[f, :, 24:32, :], 8)
    for t in range(4):
        own[t, 0:8, :] = low[t]
        own[t, 24:32, :] = high[t]
    q = [w[f] for f in range(8)]
    inv, pres = aux(q)
    gy = flux(q, inv, pres, 1)
    for f in range(8):
        fy[f] = gy[f]
    q = [w[f, :, 5:29, :] for f in range(8)]
    inv, pres = aux(q)
    gx = flux(q, inv, pres, 0)
    gz = flux(q, inv, pres, 2)
    for f in range(8):
        def y(k, f=f):
            return fy[f, :, 5 + k:29 + k, :]
        ty = combine([y(1), y(2), y(3)], [y(-1), y(-2), y(-3)])
        ty = ty + VISC * (w[f, :, 6:30, :] - 2.0 * q[f] + w[f, :, 4:28, :])
        tx = jnp.where(edge_lane, 0.0, lanes_along(gx[f], q[f]))
        s1[f, :, 0:24, :] = q[f] + tx + ty + layers_along(gz[f], q[f])

    offsets.wait()
    s_raw = jnp.clip(off_ref[0], 0, 15)
    t_raw = jnp.clip(off_ref[1] - half_offset, 0, 15)
    s_f = jnp.where(first, s_raw, zero)
    s_l = jnp.where(last, s_raw, zero)
    t_f = jnp.where(first, t_raw, zero)
    t_l = jnp.where(last, t_raw, zero)
    end_l = jnp.where(last, 1, zero)
    end_f = jnp.where(first, 1, zero)

    arrived(az.at[0:38], recv.at[R_RIGHT])
    pl.when(last)(hr_full.wait_recv)

    pl.when(even)(send_right)
    arrived(az.at[0:38], recv.at[R_LEFT])
    pl.when(first)(hl_full.wait_recv)

    pl.when(even)(send_left)

    @pl.when(edge)
    def _():
        arrived(az.at[0:32], recv.at[R_AZ])

    def jump(fields, mask_l, mask_r):
        add = jnp.where(mask_l, shear_speed, 0.0) - jnp.where(mask_r, shear_speed, 0.0)
        fields[2] = jnp.where(jnp.logical_or(mask_l, mask_r), fields[2] + add * fields[0], fields[2])

    win = 24
    hlf = bhl[1, pl.ds(5 + t_f, win), :]
    hln = bhl[0, pl.ds(5 + t_f, win), :]
    hrf = bhr[1, pl.ds(21 - t_l - end_l, win), :]
    hrn = bhr[0, pl.ds(21 - t_l - end_l, win), :]
    o_l = 21 + t_f - s_f
    ln2 = jnp.where(first, trail * az[pl.ds(o_l - end_f, win), :] + lead * az[pl.ds(o_l, win), :], own[0, 5:29, :])
    o_r = 21 - t_l - end_l + s_l
    rn2 = jnp.where(last, lead * az[pl.ds(o_r, win), :] + trail * az[pl.ds(o_r + 1, win), :], own[2, 5:29, :])
    e = [spread(f, hlf, hln, ln2, ln2, rn2, rn2, hrn, hrf) for f in range(8)]
    in_l = jnp.logical_and(cols >= 8, cols < 16)
    in_r = jnp.logical_and(cols >= 16, cols < 24)
    jump(e, jnp.logical_and(last, in_r), jnp.logical_and(first, in_l))
    inv, pres = aux(e)
    gx = flux(e, inv, pres, 0)
    gy = flux(e, inv, pres, 1)
    gz = flux(e, inv, pres, 2)
    for f in range(8):
        es[f, 0:24, :] = gy[f]
    for f in range(8):
        es[8 + f, 0:24, :] = e[f]
    strip = []
    for f in range(8):
        def y(k, f=f):
            return es[f, 3 + k:20 + k, :]
        def u(k, f=f):
            return es[8 + f, 3 + k:20 + k, :]
        ty = combine([y(1), y(2), y(3)], [y(-1), y(-2), y(-3)]) + VISC * (u(1) - 2.0 * u(0) + u(-1))
        es[16 + f, 0:24, :] = e[f] + lanes_along(gx[f], e[f]) + lane_layers_along(gz[f], e[f])
        es[16 + f, 3:20, :] = es[16 + f, 3:20, :] + ty
    at_l = jnp.logical_and(first, left_half)
    at_r = jnp.logical_and(last, jnp.logical_not(left_half))
    w_0 = jnp.where(left_half, lead, trail)
    w_1 = jnp.where(left_half, trail, lead)
    sheared = jnp.logical_or(at_l, at_r)
    for f in range(8):
        here, beyond = es[16 + f, 3:19, :], es[16 + f, 4:20, :]
        strip.append(jnp.where(sheared, w_0 * here + w_1 * beyond, here))
    jump(strip, at_l, at_r)
    packed = jnp.zeros((16, 128), jnp.float32)
    for f in range(8):
        src = jnp.where(first, strip[f], lane_roll(strip[f], -20))
        packed = jnp.where(slot_is[f], lane_roll(src, 4 * (f - 1)), packed)
    sp[...] = packed

    @pl.when(told)
    def _():
        pl.semaphore_wait(go, 1)

    @pl.when(edge)
    def _():
        swap.start()

    for f in range(8):
        es[16 + f, 0:16, :] = strip[f]

    hln0, hln1 = bhl[0, pl.ds(5 + s_f, win), :], bhl[0, pl.ds(5 + s_f + end_f, win), :]
    hln = jnp.where(first, lead * hln0 + trail * hln1, hln0)
    o_r = 21 - s_l
    hrn0, hrn1 = bhr[0, pl.ds(o_r - end_l, win), :], bhr[0, pl.ds(o_r, win), :]
    hrn = jnp.where(last, trail * hrn0 + lead * hrn1, hrn1)
    mine = [own[t, 5:29, :] for t in range(4)]
    e = [spread(f, hln, hln, mine[0], mine[1], mine[3], mine[2], hrn, hrn) for f in range(8)]
    jump(e, jnp.logical_and(first, cols < 8), jnp.logical_and(last, cols >= 24))
    inv, pres = aux(e)
    gx = flux(e, inv, pres, 0)
    for f in range(8):
        s1[f, :, 0:24, :] = s1[f, :, 0:24, :] + edges(lanes_along(gx[f], e[f]))

    q = [s1[f, :, 0:24, :] for f in range(8)]
    inv, pres = aux(q)
    gy = flux(q, inv, pres, 1)
    for f in range(8):
        fy[f, :, 0:24, :] = gy[f]
    q = [s1[f, :, 3:19, :] for f in range(8)]
    inv, pres = aux(q)
    gx = flux(q, inv, pres, 0)
    gz = flux(q, inv, pres, 2)
    tiles = pack(lambda f: q[f], 16)
    for f in range(8):
        def y(k, f=f):
            return fy[f, :, 3 + k:19 + k, :]
        ty = combine([y(1), y(2), y(3)], [y(-1), y(-2), y(-3)])
        ty = ty + VISC * (s1[f, :, 4:20, :] - 2.0 * q[f] + s1[f, :, 2:18, :])
        tx = jnp.where(edge_lane, 0.0, lanes_along(gx[f], q[f]))
        out[f] = 0.5 * w[f, :, 8:24, :] + 0.5 * (q[f] + tx + ty + layers_along(gz[f], q[f]))
    own_cols = jnp.logical_and(cols >= 8, cols < 24)
    for f in range(8):
        mid = spread(f, tiles[0], tiles[0], tiles[0], tiles[1], tiles[3], tiles[2], tiles[2], tiles[2])
        es[16 + f, 0:16, :] = jnp.where(own_cols, mid, es[16 + f, 0:16, :])

    arrived(own.at[:, 8:24], send.at[S_MAIN])
    arrived(az.at[0:12], send.at[S_CORNER])
    arrived(w.at[:, :, 0:12], send.at[S_Y])

    @pl.when(edge)
    def _():
        arrived(own.at[0:2, 8:24], send.at[S_FULL])
        arrived(az.at[0:32], send.at[S_AZ])
        swap.wait_recv()

    @pl.when(jnp.logical_and(first, jnp.logical_not(head)))
    def _():
        pl.semaphore_signal(go, inc=1, device_id=(a, r_dn), device_id_type=MESH)

    got = sq[...]
    got = jnp.where(last, lane_roll(got, 20), got)
    theirs = jnp.logical_or(jnp.logical_and(first, cols < 8), jnp.logical_and(last, cols >= 24))
    e = [jnp.where(theirs, lane_roll(got, 4 * (1 - f)), es[16 + f, 0:16, :]) for f in range(8)]
    inv, pres = aux(e)
    gx = flux(e, inv, pres, 0)
    for f in range(8):
        out[f] = out[f] + edges(0.5 * lanes_along(gx[f], e[f]))

    pl.when(edge)(swap.wait_send)


def solution(mesh):
    n_az, n_rad = mesh.shape["az"], mesh.shape["rad"]

    def shards(density, momentum, magnetic, tracer, shear_offset):
        half = n_az // 2 * density.shape[1]
        f32 = jnp.float32
        anywhere = pl.BlockSpec(memory_space=pl.ANY)
        return pl.pallas_call(
            functools.partial(kernel, n_az, n_rad, 12 if n_az % 12 == 0 else 2, half),
            out_shape=pltpu.VMEM((8, 4, 16, 128), f32),
            in_specs=[anywhere] * 5,
            out_specs=pl.BlockSpec(memory_space=pltpu.VMEM),
            scratch_shapes=[
                pltpu.SMEM((2,), jnp.int32),
                pltpu.VMEM((8, 4, 32, 128), f32),
                pltpu.VMEM((8, 4, 32, 128), f32),
                pltpu.VMEM((8, 4, 32, 128), f32),
                pltpu.VMEM((4, 32, 128), f32),
                pltpu.VMEM((2, 48, 128), f32),
                pltpu.VMEM((2, 48, 128), f32),
                pltpu.VMEM((64, 128), f32),
                pltpu.VMEM((24, 32, 128), f32),
                pltpu.VMEM((16, 128), f32),
                pltpu.VMEM((16, 128), f32),
                pltpu.SemaphoreType.DMA((2,)),
                pltpu.SemaphoreType.DMA((6,)),
                pltpu.SemaphoreType.DMA((7,)),
                pltpu.SemaphoreType.REGULAR,
            ],
            compiler_params=pltpu.CompilerParams(collective_id=0, has_side_effects=True),
        )(shear_offset, density, momentum, magnetic, tracer)

    placed = (
        P(None, "az", "rad"),
        P(None, None, "az", "rad"),
        P(None, None, "az", "rad"),
        P(None, "az", "rad"),
        P(),
    )
    return jax.shard_map(
        shards, mesh=mesh, in_specs=placed, out_specs=P(None, None, "az", "rad"), check_vma=False
    )
```

```python
import functools

import jax
import jax.numpy as jnp
from jax import lax
from jax.experimental import pallas as pl
from jax.experimental.pallas import tpu as pltpu
from jax.sharding import PartitionSpec as P

time_step = 0.025
viscosity = 0.5
sound_squared = 1.0
shear_speed = 1.0
frac_weight = 0.375

MESH = pl.DeviceIdType.MESH
D1 = -time_step * 45.0 / 60.0
D2 = time_step * 9.0 / 60.0
D3 = -time_step / 60.0
VISC = time_step * viscosity
lead = 1.0 - frac_weight
trail = frac_weight

S_MAIN, S_CORNER, S_FULL, S_AZ, S_Y, S_SWAP = range(6)
R_LEFT, R_RIGHT, R_FULL, R_AZ, R_PREV, R_NEXT, R_SWAP = range(7)


def flux(q, inv, pres, d):
    vel = [q[1 + i] * inv for i in range(3)]
    mag = q[4:7]
    vd, bd = vel[d], mag[d]
    out = [q[1 + d]]
    for i in range(3):
        g = q[1 + i] * vd - mag[i] * bd
        out.append(g + pres if i == d else g)
    for i in range(3):
        out.append(vd * mag[i] - bd * vel[i])
    out.append(q[7] * vd)
    return out


def aux(q):
    inv = 1.0 / q[0]
    pres = sound_squared * q[0] + 0.5 * (q[4] * q[4] + q[5] * q[5] + q[6] * q[6])
    return inv, pres


def combine(up, down):
    return D1 * (up[0] - down[0]) + D2 * (up[1] - down[1]) + D3 * (up[2] - down[2])


def lane_roll(x, shift):
    shift %= 128
    return x if shift == 0 else pltpu.roll(x, shift, x.ndim - 1)


def lanes_along(g, u):
    r = combine([lane_roll(g, -k) for k in (1, 2, 3)], [lane_roll(g, k) for k in (1, 2, 3)])
    return r + VISC * (lane_roll(u, -1) - 2.0 * u + lane_roll(u, 1))


def around(x, k):
    k %= x.shape[0]
    return x if k == 0 else jnp.concatenate([x[k:], x[:k]], axis=0)


def layers_along(g, u):
    r = combine([around(g, k) for k in (1, 2, 3)], [around(g, -k) for k in (1, 2, 3)])
    return r + VISC * (around(u, 1) - 2.0 * u + around(u, -1))


def lane_layers_along(g, u):
    r = combine([lane_roll(g, -32 * k) for k in (1, 2, 3)], [lane_roll(g, 32 * k) for k in (1, 2, 3)])
    return r + VISC * (lane_roll(u, -32) - 2.0 * u + lane_roll(u, 32))


def kernel(n_az, n_rad, run, half_offset, off_hbm, den, mom, mag, tra, out,
           off_ref, w, s1, fy, own, far, far_l, far_r, bhl, bhr, az, es, sp, sq, in_sem, send, recv, go):
    a = lax.axis_index("az")
    r = lax.axis_index("rad")
    first = r == 0
    last = r == n_rad - 1
    edge = jnp.logical_or(first, last)
    r_up = lax.rem(r + 1, n_rad)
    r_dn = lax.rem(r + n_rad - 1, n_rad)

    def at(step):
        return lax.rem(a + step + n_az, n_az)

    def dev(step, to_r):
        return (at(step), to_r)

    rows = pl.ds(8, 16)
    loads = [pltpu.make_async_copy(den, w.at[0, :, rows], in_sem.at[0])]
    for i in range(3):
        loads.append(pltpu.make_async_copy(mom.at[i], w.at[1 + i, :, rows], in_sem.at[0]))
        loads.append(pltpu.make_async_copy(mag.at[i], w.at[4 + i, :, rows], in_sem.at[0]))
    loads.append(pltpu.make_async_copy(tra, w.at[7, :, rows], in_sem.at[0]))
    offsets = pltpu.make_async_copy(off_hbm, off_ref, in_sem.at[1])
    for c in loads:
        c.start()
    offsets.start()

    barrier = pltpu.get_barrier_semaphore()

    def greet(step, to_r):
        pl.semaphore_signal(barrier, inc=1, device_id=dev(step, to_r), device_id_type=MESH)

    even = lax.rem(r, 2) == 0
    odd = jnp.logical_not(even)
    place = lax.rem(a, run)
    head, tail = place == 0, place == run - 1
    odd_head, odd_tail = jnp.logical_and(odd, head), jnp.logical_and(odd, tail)

    @pl.when(even)
    def _():
        for step in (-1, 0, 1):
            greet(step, r_up)
            greet(step, r_dn)

    @pl.when(first)
    def _():
        greet(2, r_dn)

    greets_half = jnp.logical_or(first, jnp.logical_and(last, head))
    told = jnp.logical_and(last, jnp.logical_not(head))

    @pl.when(greets_half)
    def _():
        greet(n_az // 2, r)

    @pl.when(jnp.logical_or(even, jnp.logical_not(tail)))
    def _():
        greet(1, r)

    @pl.when(jnp.logical_or(even, head))
    def _():
        greet(-1, r)

    w[:, :, 0:2, :] = jnp.ones((8, 4, 2, 128), jnp.float32)
    w[:, :, 30:32, :] = jnp.ones((8, 4, 2, 128), jnp.float32)
    block = w.at[:, :, rows]
    pltpu.make_async_copy(block, block, in_sem.at[0]).wait()

    lane = lax.broadcasted_iota(jnp.int32, (1, 128), 1)
    group = lane // 4
    slot_is = [lane % 32 // 4 == k for k in range(8)]
    left_half = lane % 32 < 16

    def pack(read, count):
        tiles = [jnp.zeros((count, 128), jnp.float32)] * 4
        for f in range(8):
            x = read(f)
            for z in range(4):
                moved = lane_roll(x[z], 32 * z + 4 * f)
                for t, shift in enumerate((0, 1, -1, -2)):
                    here = group == (8 * z + f + shift) % 32
                    tiles[t] = jnp.where(here, moved, tiles[t])
        return tiles

    def spread(f, hlf, hln, ln, lf, rf, rn, hrn, hrf):
        def of(k):
            return slot_is[(f + k) % 8]
        left = jnp.where(of(-2), hlf, jnp.where(of(-1), hln, jnp.where(of(0), ln, lf)))
        right = jnp.where(of(-2), rf, jnp.where(of(-1), rn, jnp.where(of(0), hrn, hrf)))
        return jnp.where(left_half, lane_roll(left, 4 * (2 - f)), lane_roll(right, 4 * (6 - f)))

    tiles = pack(lambda f: w[f, :, 8:24, :], 16)
    for t in range(4):
        own[t, 8:24, :] = tiles[t]
    inner_two = lane % 4 < 2
    far[0] = jnp.where(inner_two, tiles[1][0:8], lane_roll(tiles[1][8:16], 2))
    far[1] = jnp.where(inner_two, lane_roll(tiles[3][8:16], -2), tiles[3][0:8])
    az[24:40, :] = jnp.where(first, tiles[0], tiles[2])

    one = jnp.int32(1)
    zero = jnp.int32(0)
    along = jnp.where(even, 2 * one, jnp.where(head, zero, jnp.where(tail, 2 * one, one)))
    across = jnp.where(even, zero, jnp.where(last, 7 * one, 6 * one))
    pl.semaphore_wait(barrier, along + across + jnp.where(greets_half, one, zero))

    def remote(k, n, src, dst, step, to_r):
        return pltpu.make_async_remote_copy(
            src_ref=src, dst_ref=dst, send_sem=send.at[k], recv_sem=recv.at[n],
            device_id=dev(step, to_r), device_id_type=MESH)

    def arrived(ref, sem):
        pltpu.make_async_copy(ref, ref, sem).wait()

    own_l, own_r = own.at[0, 8:24], own.at[2, 8:24]
    ln, rn = own.at[0], own.at[2]
    hl_main = (remote(S_MAIN, R_LEFT, own_r, bhl.at[0, 8:24], 0, r_up),
               remote(S_MAIN, R_LEFT, far.at[1], far_l.at[0], 0, r_up))
    hr_main = (remote(S_MAIN, R_RIGHT, own_l, bhr.at[0, 24:40], 0, r_dn),
               remote(S_MAIN, R_RIGHT, far.at[0], far_r.at[0], 0, r_dn))
    hl_full = (remote(S_FULL, R_FULL, own_r, bhl.at[0, 24:40], -1, r_up),
               remote(S_FULL, R_FULL, far.at[1], far_l.at[1], -1, r_up))
    hr_full = (remote(S_FULL, R_FULL, own_l, bhr.at[0, 8:24], 1, r_dn),
               remote(S_FULL, R_FULL, far.at[0], far_r.at[1], 1, r_dn))
    hl_prev = remote(S_CORNER, R_LEFT, rn.at[21:24], bhl.at[0, 5:8], 1, r_up)
    hr_next = remote(S_CORNER, R_RIGHT, ln.at[8:11], bhr.at[0, 40:43], -1, r_dn)
    hl_next_in = remote(S_CORNER, R_LEFT, rn.at[8:11], bhl.at[0, 24:27], -1, r_up)
    hl_next_end = remote(S_CORNER, R_LEFT, rn.at[8:11], bhl.at[0, 40:43], -2, r_up)
    hr_prev_in = remote(S_CORNER, R_RIGHT, ln.at[21:24], bhr.at[0, 21:24], 1, r_dn)
    hr_prev_end = remote(S_CORNER, R_RIGHT, ln.at[21:24], bhr.at[0, 5:8], 2, r_dn)
    az_prev = remote(S_AZ, R_AZ, az.at[24:40], az.at[8:24], 1, r)
    az_next = remote(S_AZ, R_AZ, az.at[24:40], az.at[40:56], -1, r)
    y_prev = remote(S_Y, R_PREV, w.at[:, :, 18:24], w.at[:, :, 2:8], 1, r)
    y_next = remote(S_Y, R_NEXT, w.at[:, :, 8:14], w.at[:, :, 24:30], -1, r)
    swap = remote(S_SWAP, R_SWAP, sp, sq, n_az // 2, r)

    def send_right():
        for c in hl_main:
            c.start()

        @pl.when(last)
        def _():
            for c in hl_full:
                c.start()
            hl_next_end.start()

        @pl.when(jnp.logical_not(last))
        def _():
            hl_next_in.start()

        hl_prev.start()

    def send_left():
        for c in hr_main:
            c.start()

        @pl.when(first)
        def _():
            for c in hr_full:
                c.start()
            hr_prev_end.start()

        @pl.when(jnp.logical_not(first))
        def _():
            hr_prev_in.start()

        hr_next.start()

    def send_up():
        @pl.when(edge)
        def _():
            az_prev.start()
        y_prev.start()

    def send_down():
        @pl.when(edge)
        def _():
            az_next.start()
        y_next.start()

    @pl.when(odd)
    def _():
        send_right()
        send_left()
        arrived(az.at[0:48], send.at[S_MAIN])

    pl.when(jnp.logical_or(even, tail))(send_up)
    pl.when(jnp.logical_not(odd_head))(send_down)

    @pl.when(jnp.logical_and(odd, jnp.logical_not(tail)))
    def _():
        y_next.wait_recv()
        send_up()

    @pl.when(odd_head)
    def _():
        y_prev.wait_recv()
        send_down()

    @pl.when(jnp.logical_or(even, tail))
    def _():
        y_next.wait_recv()

    @pl.when(jnp.logical_not(odd_head))
    def _():
        y_prev.wait_recv()

    cols = lane % 32

    edge_lane = jnp.logical_or(lane < 3, lane >= 125)

    def edges(strip_f):
        joined = jnp.where(jnp.logical_and(cols >= 5, cols < 8), lane_roll(strip_f, -16), strip_f)
        return jnp.stack([jnp.where(edge_lane, lane_roll(joined, -(32 * z + 8)), 0.0) for z in range(4)])

    low = pack(lambda f: w[f, :, 0:8, :], 8)
    high = pack(lambda f: w[f, :, 24:32, :], 8)
    for t in range(4):
        own[t, 0:8, :] = low[t]
        own[t, 24:32, :] = high[t]
    q = [w[f] for f in range(8)]
    inv, pres = aux(q)
    gy = flux(q, inv, pres, 1)
    for f in range(8):
        fy[f] = gy[f]
    q = [w[f, :, 5:29, :] for f in range(8)]
    inv, pres = aux(q)
    gx = flux(q, inv, pres, 0)
    gz = flux(q, inv, pres, 2)
    for f in range(8):
        def y(k, f=f):
            return fy[f, :, 5 + k:29 + k, :]
        ty = combine([y(1), y(2), y(3)], [y(-1), y(-2), y(-3)])
        ty = ty + VISC * (w[f, :, 6:30, :] - 2.0 * q[f] + w[f, :, 4:28, :])
        tx = jnp.where(edge_lane, 0.0, lanes_along(gx[f], q[f]))
        s1[f, :, 0:24, :] = q[f] + tx + ty + layers_along(gz[f], q[f])

    offsets.wait()
    s_raw = jnp.clip(off_ref[0], 0, 15)
    t_raw = jnp.clip(off_ref[1] - half_offset, 0, 15)
    s_f = jnp.where(first, s_raw, zero)
    s_l = jnp.where(last, s_raw, zero)
    t_f = jnp.where(first, t_raw, zero)
    t_l = jnp.where(last, t_raw, zero)
    end_l = jnp.where(last, 1, zero)
    end_f = jnp.where(first, 1, zero)

    arrived(az.at[0:30], recv.at[R_RIGHT])

    @pl.when(last)
    def _():
        arrived(az.at[0:24], recv.at[R_FULL])

    pl.when(even)(send_right)
    arrived(az.at[0:30], recv.at[R_LEFT])

    @pl.when(first)
    def _():
        arrived(az.at[0:24], recv.at[R_FULL])

    pl.when(even)(send_left)

    @pl.when(edge)
    def _():
        arrived(az.at[0:32], recv.at[R_AZ])

    def jump(fields, mask_l, mask_r):
        add = jnp.where(mask_l, shear_speed, 0.0) - jnp.where(mask_r, shear_speed, 0.0)
        fields[2] = jnp.where(jnp.logical_or(mask_l, mask_r), fields[2] + add * fields[0], fields[2])

    win = 24
    for k, row in ((0, 8), (1, 24)):
        bhl[1, row:row + 8, :] = far_l[k]
        bhl[1, row + 8:row + 16, :] = lane_roll(far_l[k], 2)
        bhr[1, 32 - row:40 - row, :] = far_r[k]
        bhr[1, 40 - row:48 - row, :] = lane_roll(far_r[k], -2)
    hlf = bhl[1, pl.ds(5 + t_f, win), :]
    hln = bhl[0, pl.ds(5 + t_f, win), :]
    hrf = bhr[1, pl.ds(21 - t_l - end_l, win), :]
    hrn = bhr[0, pl.ds(21 - t_l - end_l, win), :]
    o_l = 21 + t_f - s_f
    ln2 = jnp.where(first, trail * az[pl.ds(o_l - end_f, win), :] + lead * az[pl.ds(o_l, win), :], own[0, 5:29, :])
    o_r = 21 - t_l - end_l + s_l
    rn2 = jnp.where(last, lead * az[pl.ds(o_r, win), :] + trail * az[pl.ds(o_r + 1, win), :], own[2, 5:29, :])
    e = [spread(f, hlf, hln, ln2, ln2, rn2, rn2, hrn, hrf) for f in range(8)]
    in_l = jnp.logical_and(cols >= 8, cols < 16)
    in_r = jnp.logical_and(cols >= 16, cols < 24)
    jump(e, jnp.logical_and(last, in_r), jnp.logical_and(first, in_l))
    inv, pres = aux(e)
    gx = flux(e, inv, pres, 0)
    gy = flux(e, inv, pres, 1)
    gz = flux(e, inv, pres, 2)
    for f in range(8):
        es[f, 0:24, :] = gy[f]
    for f in range(8):
        es[8 + f, 0:24, :] = e[f]
    strip = []
    for f in range(8):
        def y(k, f=f):
            return es[f, 3 + k:20 + k, :]
        def u(k, f=f):
            return es[8 + f, 3 + k:20 + k, :]
        ty = combine([y(1), y(2), y(3)], [y(-1), y(-2), y(-3)]) + VISC * (u(1) - 2.0 * u(0) + u(-1))
        es[16 + f, 0:24, :] = e[f] + lanes_along(gx[f], e[f]) + lane_layers_along(gz[f], e[f])
        es[16 + f, 3:20, :] = es[16 + f, 3:20, :] + ty
    at_l = jnp.logical_and(first, left_half)
    at_r = jnp.logical_and(last, jnp.logical_not(left_half))
    w_0 = jnp.where(left_half, lead, trail)
    w_1 = jnp.where(left_half, trail, lead)
    sheared = jnp.logical_or(at_l, at_r)
    for f in range(8):
        here, beyond = es[16 + f, 3:19, :], es[16 + f, 4:20, :]
        strip.append(jnp.where(sheared, w_0 * here + w_1 * beyond, here))
    jump(strip, at_l, at_r)
    packed = jnp.zeros((16, 128), jnp.float32)
    for f in range(8):
        src = jnp.where(first, strip[f], lane_roll(strip[f], -20))
        packed = jnp.where(slot_is[f], lane_roll(src, 4 * (f - 1)), packed)
    sp[...] = packed

    @pl.when(told)
    def _():
        pl.semaphore_wait(go, 1)

    @pl.when(edge)
    def _():
        swap.start()

    for f in range(8):
        es[16 + f, 0:16, :] = strip[f]

    hln0, hln1 = bhl[0, pl.ds(5 + s_f, win), :], bhl[0, pl.ds(5 + s_f + end_f, win), :]
    hln = jnp.where(first, lead * hln0 + trail * hln1, hln0)
    o_r = 21 - s_l
    hrn0, hrn1 = bhr[0, pl.ds(o_r - end_l, win), :], bhr[0, pl.ds(o_r, win), :]
    hrn = jnp.where(last, trail * hrn0 + lead * hrn1, hrn1)
    mine = [own[t, 5:29, :] for t in range(4)]
    e = [spread(f, hln, hln, mine[0], mine[1], mine[3], mine[2], hrn, hrn) for f in range(8)]
    jump(e, jnp.logical_and(first, cols < 8), jnp.logical_and(last, cols >= 24))
    inv, pres = aux(e)
    gx = flux(e, inv, pres, 0)
    for f in range(8):
        s1[f, :, 0:24, :] = s1[f, :, 0:24, :] + edges(lanes_along(gx[f], e[f]))

    q = [s1[f, :, 0:24, :] for f in range(8)]
    inv, pres = aux(q)
    gy = flux(q, inv, pres, 1)
    for f in range(8):
        fy[f, :, 0:24, :] = gy[f]
    q = [s1[f, :, 3:19, :] for f in range(8)]
    inv, pres = aux(q)
    gx = flux(q, inv, pres, 0)
    gz = flux(q, inv, pres, 2)
    tiles = pack(lambda f: q[f], 16)
    for f in range(8):
        def y(k, f=f):
            return fy[f, :, 3 + k:19 + k, :]
        ty = combine([y(1), y(2), y(3)], [y(-1), y(-2), y(-3)])
        ty = ty + VISC * (s1[f, :, 4:20, :] - 2.0 * q[f] + s1[f, :, 2:18, :])
        tx = jnp.where(edge_lane, 0.0, lanes_along(gx[f], q[f]))
        out[f] = 0.5 * w[f, :, 8:24, :] + 0.5 * (q[f] + tx + ty + layers_along(gz[f], q[f]))
    own_cols = jnp.logical_and(cols >= 8, cols < 24)
    for f in range(8):
        mid = spread(f, tiles[0], tiles[0], tiles[0], tiles[1], tiles[3], tiles[2], tiles[2], tiles[2])
        es[16 + f, 0:16, :] = jnp.where(own_cols, mid, es[16 + f, 0:16, :])

    @pl.when(even)
    def _():
        arrived(az.at[0:48], send.at[S_MAIN])

    arrived(az.at[0:12], send.at[S_CORNER])
    arrived(w.at[:, :, 0:12], send.at[S_Y])

    @pl.when(edge)
    def _():
        arrived(az.at[0:24], send.at[S_FULL])
        arrived(az.at[0:32], send.at[S_AZ])
        swap.wait_recv()

    @pl.when(jnp.logical_and(first, jnp.logical_not(head)))
    def _():
        pl.semaphore_signal(go, inc=1, device_id=(a, r_dn), device_id_type=MESH)

    got = sq[...]
    got = jnp.where(last, lane_roll(got, 20), got)
    theirs = jnp.logical_or(jnp.logical_and(first, cols < 8), jnp.logical_and(last, cols >= 24))
    e = [jnp.where(theirs, lane_roll(got, 4 * (1 - f)), es[16 + f, 0:16, :]) for f in range(8)]
    inv, pres = aux(e)
    gx = flux(e, inv, pres, 0)
    for f in range(8):
        out[f] = out[f] + edges(0.5 * lanes_along(gx[f], e[f]))

    pl.when(edge)(swap.wait_send)


def solution(mesh):
    n_az, n_rad = mesh.shape["az"], mesh.shape["rad"]

    def shards(density, momentum, magnetic, tracer, shear_offset):
        half = n_az // 2 * density.shape[1]
        f32 = jnp.float32
        anywhere = pl.BlockSpec(memory_space=pl.ANY)
        return pl.pallas_call(
            functools.partial(kernel, n_az, n_rad, 12 if n_az % 12 == 0 else 2, half),
            out_shape=pltpu.VMEM((8, 4, 16, 128), f32),
            in_specs=[anywhere] * 5,
            out_specs=pl.BlockSpec(memory_space=pltpu.VMEM),
            scratch_shapes=[
                pltpu.SMEM((2,), jnp.int32),
                pltpu.VMEM((8, 4, 32, 128), f32),
                pltpu.VMEM((8, 4, 32, 128), f32),
                pltpu.VMEM((8, 4, 32, 128), f32),
                pltpu.VMEM((4, 32, 128), f32),
                pltpu.VMEM((2, 8, 128), f32),
                pltpu.VMEM((2, 8, 128), f32),
                pltpu.VMEM((2, 8, 128), f32),
                pltpu.VMEM((2, 48, 128), f32),
                pltpu.VMEM((2, 48, 128), f32),
                pltpu.VMEM((64, 128), f32),
                pltpu.VMEM((24, 32, 128), f32),
                pltpu.VMEM((16, 128), f32),
                pltpu.VMEM((16, 128), f32),
                pltpu.SemaphoreType.DMA((2,)),
                pltpu.SemaphoreType.DMA((6,)),
                pltpu.SemaphoreType.DMA((7,)),
                pltpu.SemaphoreType.REGULAR,
            ],
            compiler_params=pltpu.CompilerParams(collective_id=0, has_side_effects=True),
        )(shear_offset, density, momentum, magnetic, tracer)

    placed = (
        P(None, "az", "rad"),
        P(None, None, "az", "rad"),
        P(None, None, "az", "rad"),
        P(None, "az", "rad"),
        P(),
    )
    return jax.shard_map(
        shards, mesh=mesh, in_specs=placed, out_specs=P(None, None, "az", "rad"), check_vma=False
    )
```

```python
import functools

import jax
import jax.numpy as jnp
from jax import lax
from jax.experimental import pallas as pl
from jax.experimental.pallas import tpu as pltpu
from jax.sharding import PartitionSpec as P

time_step = 0.025
viscosity = 0.5
sound_squared = 1.0
shear_speed = 1.0
frac_weight = 0.375

MESH = pl.DeviceIdType.MESH
D1 = -time_step * 45.0 / 60.0
D2 = time_step * 9.0 / 60.0
D3 = -time_step / 60.0
VISC = time_step * viscosity
lead = 1.0 - frac_weight
trail = frac_weight

S_MAIN, S_CORNER, S_FULL, S_AZ, S_Y, S_SWAP = range(6)
R_LEFT, R_RIGHT, R_FULL, R_AZ, R_PREV, R_NEXT, R_SWAP = range(7)


def flux(q, inv, pres, d):
    vel = [q[1 + i] * inv for i in range(3)]
    mag = q[4:7]
    vd, bd = vel[d], mag[d]
    out = [q[1 + d]]
    for i in range(3):
        g = q[1 + i] * vd - mag[i] * bd
        out.append(g + pres if i == d else g)
    for i in range(3):
        out.append(vd * mag[i] - bd * vel[i])
    out.append(q[7] * vd)
    return out


def aux(q):
    inv = 1.0 / q[0]
    pres = sound_squared * q[0] + 0.5 * (q[4] * q[4] + q[5] * q[5] + q[6] * q[6])
    return inv, pres


def combine(up, down):
    return D1 * (up[0] - down[0]) + D2 * (up[1] - down[1]) + D3 * (up[2] - down[2])


def lane_roll(x, shift):
    shift %= 128
    return x if shift == 0 else pltpu.roll(x, shift, x.ndim - 1)


def lanes_along(g, u):
    r = combine([lane_roll(g, -k) for k in (1, 2, 3)], [lane_roll(g, k) for k in (1, 2, 3)])
    return r + VISC * (lane_roll(u, -1) - 2.0 * u + lane_roll(u, 1))


def around(x, k):
    k %= x.shape[0]
    return x if k == 0 else jnp.concatenate([x[k:], x[:k]], axis=0)


def layers_along(g, u):
    r = combine([around(g, k) for k in (1, 2, 3)], [around(g, -k) for k in (1, 2, 3)])
    return r + VISC * (around(u, 1) - 2.0 * u + around(u, -1))


def lane_layers_along(g, u):
    r = combine([lane_roll(g, -32 * k) for k in (1, 2, 3)], [lane_roll(g, 32 * k) for k in (1, 2, 3)])
    return r + VISC * (lane_roll(u, -32) - 2.0 * u + lane_roll(u, 32))


def kernel(n_az, n_rad, run, half_offset, off_hbm, den, mom, mag, tra, out,
           off_ref, w, s1, fy, own, far, far_l, far_r, bhl, bhr, az, es, sp, sq, in_sem, send, recv, go):
    a = lax.axis_index("az")
    r = lax.axis_index("rad")
    first = r == 0
    last = r == n_rad - 1
    edge = jnp.logical_or(first, last)
    r_up = lax.rem(r + 1, n_rad)
    r_dn = lax.rem(r + n_rad - 1, n_rad)

    def at(step):
        return lax.rem(a + step + n_az, n_az)

    def dev(step, to_r):
        return (at(step), to_r)

    rows = pl.ds(8, 16)
    loads = [pltpu.make_async_copy(den, w.at[0, :, rows], in_sem.at[0])]
    for i in range(3):
        loads.append(pltpu.make_async_copy(mom.at[i], w.at[1 + i, :, rows], in_sem.at[0]))
        loads.append(pltpu.make_async_copy(mag.at[i], w.at[4 + i, :, rows], in_sem.at[0]))
    loads.append(pltpu.make_async_copy(tra, w.at[7, :, rows], in_sem.at[0]))
    offsets = pltpu.make_async_copy(off_hbm, off_ref, in_sem.at[1])
    for c in loads:
        c.start()
    offsets.start()

    barrier = pltpu.get_barrier_semaphore()

    def greet(step, to_r):
        pl.semaphore_signal(barrier, inc=1, device_id=dev(step, to_r), device_id_type=MESH)

    even = lax.rem(r, 2) == 0
    odd = jnp.logical_not(even)
    place = lax.rem(a, run)
    head, tail = place == 0, place == run - 1
    odd_head, odd_tail = jnp.logical_and(odd, head), jnp.logical_and(odd, tail)

    @pl.when(even)
    def _():
        for step in (-1, 0, 1):
            greet(step, r_up)
            greet(step, r_dn)

    @pl.when(first)
    def _():
        greet(2, r_dn)

    greets_half = jnp.logical_or(first, jnp.logical_and(last, head))
    told = jnp.logical_and(last, jnp.logical_not(head))

    @pl.when(greets_half)
    def _():
        greet(n_az // 2, r)

    @pl.when(jnp.logical_or(even, jnp.logical_not(tail)))
    def _():
        greet(1, r)

    @pl.when(jnp.logical_or(even, head))
    def _():
        greet(-1, r)

    w[:, :, 0:2, :] = jnp.ones((8, 4, 2, 128), jnp.float32)
    w[:, :, 30:32, :] = jnp.ones((8, 4, 2, 128), jnp.float32)
    block = w.at[:, :, rows]
    pltpu.make_async_copy(block, block, in_sem.at[0]).wait()

    lane = lax.broadcasted_iota(jnp.int32, (1, 128), 1)
    group = lane // 4
    slot_is = [lane % 32 // 4 == k for k in range(8)]
    left_half = lane % 32 < 16

    def pack(read, count):
        tiles = [jnp.zeros((count, 128), jnp.float32)] * 4
        for f in range(8):
            x = read(f)
            for z in range(4):
                moved = lane_roll(x[z], 32 * z + 4 * f)
                for t, shift in enumerate((0, 1, -1, -2)):
                    here = group == (8 * z + f + shift) % 32
                    tiles[t] = jnp.where(here, moved, tiles[t])
        return tiles

    def spread(f, hlf, hln, ln, lf, rf, rn, hrn, hrf):
        def of(k):
            return slot_is[(f + k) % 8]
        left = jnp.where(of(-2), hlf, jnp.where(of(-1), hln, jnp.where(of(0), ln, lf)))
        right = jnp.where(of(-2), rf, jnp.where(of(-1), rn, jnp.where(of(0), hrn, hrf)))
        return jnp.where(left_half, lane_roll(left, 4 * (2 - f)), lane_roll(right, 4 * (6 - f)))

    tiles = pack(lambda f: w[f, :, 8:24, :], 16)
    for t in range(4):
        own[t, 8:24, :] = tiles[t]
    inner_two = lane % 4 < 2
    far[0] = jnp.where(inner_two, tiles[1][0:8], lane_roll(tiles[1][8:16], 2))
    far[1] = jnp.where(inner_two, lane_roll(tiles[3][8:16], -2), tiles[3][0:8])
    az[24:40, :] = jnp.where(first, tiles[0], tiles[2])

    one = jnp.int32(1)
    zero = jnp.int32(0)
    along = jnp.where(even, 2 * one, jnp.where(head, zero, jnp.where(tail, 2 * one, one)))
    across = jnp.where(even, zero, jnp.where(last, 7 * one, 6 * one))
    pl.semaphore_wait(barrier, along + across + jnp.where(greets_half, one, zero))

    def remote(k, n, src, dst, step, to_r):
        return pltpu.make_async_remote_copy(
            src_ref=src, dst_ref=dst, send_sem=send.at[k], recv_sem=recv.at[n],
            device_id=dev(step, to_r), device_id_type=MESH)

    def arrived(ref, sem):
        pltpu.make_async_copy(ref, ref, sem).wait()

    own_l, own_r = own.at[0, 8:24], own.at[2, 8:24]
    ln, rn = own.at[0], own.at[2]
    hl_main = (remote(S_MAIN, R_LEFT, own_r, bhl.at[0, 8:24], 0, r_up),
               remote(S_MAIN, R_LEFT, far.at[1], far_l.at[0], 0, r_up))
    hr_main = (remote(S_MAIN, R_RIGHT, own_l, bhr.at[0, 24:40], 0, r_dn),
               remote(S_MAIN, R_RIGHT, far.at[0], far_r.at[0], 0, r_dn))
    hl_full = (remote(S_FULL, R_FULL, own_r, bhl.at[0, 24:40], -1, r_up),
               remote(S_FULL, R_FULL, far.at[1], far_l.at[1], -1, r_up))
    hr_full = (remote(S_FULL, R_FULL, own_l, bhr.at[0, 8:24], 1, r_dn),
               remote(S_FULL, R_FULL, far.at[0], far_r.at[1], 1, r_dn))
    hl_prev = remote(S_CORNER, R_LEFT, rn.at[21:24], bhl.at[0, 5:8], 1, r_up)
    hr_next = remote(S_CORNER, R_RIGHT, ln.at[8:11], bhr.at[0, 40:43], -1, r_dn)
    hl_next_in = remote(S_CORNER, R_LEFT, rn.at[8:11], bhl.at[0, 24:27], -1, r_up)
    hl_next_end = remote(S_CORNER, R_LEFT, rn.at[8:11], bhl.at[0, 40:43], -2, r_up)
    hr_prev_in = remote(S_CORNER, R_RIGHT, ln.at[21:24], bhr.at[0, 21:24], 1, r_dn)
    hr_prev_end = remote(S_CORNER, R_RIGHT, ln.at[21:24], bhr.at[0, 5:8], 2, r_dn)
    az_prev = remote(S_AZ, R_AZ, az.at[24:40], az.at[8:24], 1, r)
    az_next = remote(S_AZ, R_AZ, az.at[24:40], az.at[40:56], -1, r)
    y_prev = remote(S_Y, R_PREV, w.at[:, :, 18:24], w.at[:, :, 2:8], 1, r)
    y_next = remote(S_Y, R_NEXT, w.at[:, :, 8:14], w.at[:, :, 24:30], -1, r)
    swap = remote(S_SWAP, R_SWAP, sp, sq, n_az // 2, r)

    def send_right():
        for c in hl_main:
            c.start()

        @pl.when(last)
        def _():
            for c in hl_full:
                c.start()
            hl_next_end.start()

        @pl.when(jnp.logical_not(last))
        def _():
            hl_next_in.start()

        hl_prev.start()

    def send_left():
        for c in hr_main:
            c.start()

        @pl.when(first)
        def _():
            for c in hr_full:
                c.start()
            hr_prev_end.start()

        @pl.when(jnp.logical_not(first))
        def _():
            hr_prev_in.start()

        hr_next.start()

    def send_up():
        @pl.when(edge)
        def _():
            az_prev.start()
        y_prev.start()

    def send_down():
        @pl.when(edge)
        def _():
            az_next.start()
        y_next.start()

    @pl.when(odd)
    def _():
        send_right()
        send_left()
        arrived(az.at[0:48], send.at[S_MAIN])

    pl.when(jnp.logical_or(even, tail))(send_up)
    pl.when(jnp.logical_not(odd_head))(send_down)

    @pl.when(jnp.logical_and(odd, jnp.logical_not(tail)))
    def _():
        y_next.wait_recv()
        send_up()

    @pl.when(odd_head)
    def _():
        y_prev.wait_recv()
        send_down()

    @pl.when(jnp.logical_or(even, tail))
    def _():
        y_next.wait_recv()

    @pl.when(jnp.logical_not(odd_head))
    def _():
        y_prev.wait_recv()

    cols = lane % 32

    edge_lane = jnp.logical_or(lane < 3, lane >= 125)

    def edges(strip_f):
        joined = jnp.where(jnp.logical_and(cols >= 5, cols < 8), lane_roll(strip_f, -16), strip_f)
        return jnp.stack([jnp.where(edge_lane, lane_roll(joined, -(32 * z + 8)), 0.0) for z in range(4)])

    low = pack(lambda f: w[f, :, 0:8, :], 8)
    high = pack(lambda f: w[f, :, 24:32, :], 8)
    for t in range(4):
        own[t, 0:8, :] = low[t]
        own[t, 24:32, :] = high[t]
    q = [w[f] for f in range(8)]
    inv, pres = aux(q)
    gy = flux(q, inv, pres, 1)
    for f in range(8):
        fy[f] = gy[f]
    q = [w[f, :, 5:29, :] for f in range(8)]
    inv, pres = aux(q)
    gx = flux(q, inv, pres, 0)
    gz = flux(q, inv, pres, 2)
    for f in range(8):
        def y(k, f=f):
            return fy[f, :, 5 + k:29 + k, :]
        ty = combine([y(1), y(2), y(3)], [y(-1), y(-2), y(-3)])
        ty = ty + VISC * (w[f, :, 6:30, :] - 2.0 * q[f] + w[f, :, 4:28, :])
        tx = jnp.where(edge_lane, 0.0, lanes_along(gx[f], q[f]))
        s1[f, :, 0:24, :] = q[f] + tx + ty + layers_along(gz[f], q[f])

    offsets.wait()
    s_raw = jnp.clip(off_ref[0], 0, 15)
    t_raw = jnp.clip(off_ref[1] - half_offset, 0, 15)
    s_f = jnp.where(first, s_raw, zero)
    s_l = jnp.where(last, s_raw, zero)
    t_f = jnp.where(first, t_raw, zero)
    t_l = jnp.where(last, t_raw, zero)
    end_l = jnp.where(last, 1, zero)
    end_f = jnp.where(first, 1, zero)

    arrived(az.at[0:30], recv.at[R_RIGHT])

    @pl.when(last)
    def _():
        arrived(az.at[0:24], recv.at[R_FULL])

    pl.when(even)(send_right)
    arrived(az.at[0:30], recv.at[R_LEFT])

    @pl.when(first)
    def _():
        arrived(az.at[0:24], recv.at[R_FULL])


    @pl.when(edge)
    def _():
        arrived(az.at[0:32], recv.at[R_AZ])

    def jump(fields, mask_l, mask_r):
        add = jnp.where(mask_l, shear_speed, 0.0) - jnp.where(mask_r, shear_speed, 0.0)
        fields[2] = jnp.where(jnp.logical_or(mask_l, mask_r), fields[2] + add * fields[0], fields[2])

    win = 24
    for k, row in ((0, 8), (1, 24)):
        bhl[1, row:row + 8, :] = far_l[k]
        bhl[1, row + 8:row + 16, :] = lane_roll(far_l[k], 2)
        bhr[1, 32 - row:40 - row, :] = far_r[k]
        bhr[1, 40 - row:48 - row, :] = lane_roll(far_r[k], -2)
    hlf = bhl[1, pl.ds(5 + t_f, win), :]
    hln = bhl[0, pl.ds(5 + t_f, win), :]
    hrf = bhr[1, pl.ds(21 - t_l - end_l, win), :]
    hrn = bhr[0, pl.ds(21 - t_l - end_l, win), :]
    o_l = 21 + t_f - s_f
    ln2 = jnp.where(first, trail * az[pl.ds(o_l - end_f, win), :] + lead * az[pl.ds(o_l, win), :], own[0, 5:29, :])
    o_r = 21 - t_l - end_l + s_l
    rn2 = jnp.where(last, lead * az[pl.ds(o_r, win), :] + trail * az[pl.ds(o_r + 1, win), :], own[2, 5:29, :])
    e = [spread(f, hlf, hln, ln2, ln2, rn2, rn2, hrn, hrf) for f in range(8)]
    in_l = jnp.logical_and(cols >= 8, cols < 16)
    in_r = jnp.logical_and(cols >= 16, cols < 24)
    jump(e, jnp.logical_and(last, in_r), jnp.logical_and(first, in_l))
    inv, pres = aux(e)
    gx = flux(e, inv, pres, 0)
    gy = flux(e, inv, pres, 1)
    gz = flux(e, inv, pres, 2)
    for f in range(8):
        es[f, 0:24, :] = gy[f]
    for f in range(8):
        es[8 + f, 0:24, :] = e[f]
    strip = []
    for f in range(8):
        def y(k, f=f):
            return es[f, 3 + k:20 + k, :]
        def u(k, f=f):
            return es[8 + f, 3 + k:20 + k, :]
        ty = combine([y(1), y(2), y(3)], [y(-1), y(-2), y(-3)]) + VISC * (u(1) - 2.0 * u(0) + u(-1))
        es[16 + f, 0:24, :] = e[f] + lanes_along(gx[f], e[f]) + lane_layers_along(gz[f], e[f])
        es[16 + f, 3:20, :] = es[16 + f, 3:20, :] + ty
    at_l = jnp.logical_and(first, left_half)
    at_r = jnp.logical_and(last, jnp.logical_not(left_half))
    w_0 = jnp.where(left_half, lead, trail)
    w_1 = jnp.where(left_half, trail, lead)
    sheared = jnp.logical_or(at_l, at_r)
    for f in range(8):
        here, beyond = es[16 + f, 3:19, :], es[16 + f, 4:20, :]
        strip.append(jnp.where(sheared, w_0 * here + w_1 * beyond, here))
    jump(strip, at_l, at_r)
    packed = jnp.zeros((16, 128), jnp.float32)
    for f in range(8):
        src = jnp.where(first, strip[f], lane_roll(strip[f], -20))
        packed = jnp.where(slot_is[f], lane_roll(src, 4 * (f - 1)), packed)
    sp[...] = packed

    @pl.when(told)
    def _():
        pl.semaphore_wait(go, 1)

    @pl.when(edge)
    def _():
        swap.start()

    pl.when(even)(send_left)

    for f in range(8):
        es[16 + f, 0:16, :] = strip[f]

    hln0, hln1 = bhl[0, pl.ds(5 + s_f, win), :], bhl[0, pl.ds(5 + s_f + end_f, win), :]
    hln = jnp.where(first, lead * hln0 + trail * hln1, hln0)
    o_r = 21 - s_l
    hrn0, hrn1 = bhr[0, pl.ds(o_r - end_l, win), :], bhr[0, pl.ds(o_r, win), :]
    hrn = jnp.where(last, trail * hrn0 + lead * hrn1, hrn1)
    mine = [own[t, 5:29, :] for t in range(4)]
    e = [spread(f, hln, hln, mine[0], mine[1], mine[3], mine[2], hrn, hrn) for f in range(8)]
    jump(e, jnp.logical_and(first, cols < 8), jnp.logical_and(last, cols >= 24))
    inv, pres = aux(e)
    gx = flux(e, inv, pres, 0)
    for f in range(8):
        s1[f, :, 0:24, :] = s1[f, :, 0:24, :] + edges(lanes_along(gx[f], e[f]))

    q = [s1[f, :, 0:24, :] for f in range(8)]
    inv, pres = aux(q)
    gy = flux(q, inv, pres, 1)
    for f in range(8):
        fy[f, :, 0:24, :] = gy[f]
    q = [s1[f, :, 3:19, :] for f in range(8)]
    inv, pres = aux(q)
    gx = flux(q, inv, pres, 0)
    gz = flux(q, inv, pres, 2)
    tiles = pack(lambda f: q[f], 16)
    for f in range(8):
        def y(k, f=f):
            return fy[f, :, 3 + k:19 + k, :]
        ty = combine([y(1), y(2), y(3)], [y(-1), y(-2), y(-3)])
        ty = ty + VISC * (s1[f, :, 4:20, :] - 2.0 * q[f] + s1[f, :, 2:18, :])
        tx = jnp.where(edge_lane, 0.0, lanes_along(gx[f], q[f]))
        out[f] = 0.5 * w[f, :, 8:24, :] + 0.5 * (q[f] + tx + ty + layers_along(gz[f], q[f]))
    own_cols = jnp.logical_and(cols >= 8, cols < 24)
    for f in range(8):
        mid = spread(f, tiles[0], tiles[0], tiles[0], tiles[1], tiles[3], tiles[2], tiles[2], tiles[2])
        es[16 + f, 0:16, :] = jnp.where(own_cols, mid, es[16 + f, 0:16, :])

    @pl.when(even)
    def _():
        arrived(az.at[0:48], send.at[S_MAIN])

    arrived(az.at[0:12], send.at[S_CORNER])
    arrived(w.at[:, :, 0:12], send.at[S_Y])

    @pl.when(edge)
    def _():
        arrived(az.at[0:24], send.at[S_FULL])
        arrived(az.at[0:32], send.at[S_AZ])
        swap.wait_recv()

    @pl.when(jnp.logical_and(first, jnp.logical_not(head)))
    def _():
        pl.semaphore_signal(go, inc=1, device_id=(a, r_dn), device_id_type=MESH)

    got = sq[...]
    got = jnp.where(last, lane_roll(got, 20), got)
    theirs = jnp.logical_or(jnp.logical_and(first, cols < 8), jnp.logical_and(last, cols >= 24))
    e = [jnp.where(theirs, lane_roll(got, 4 * (1 - f)), es[16 + f, 0:16, :]) for f in range(8)]
    inv, pres = aux(e)
    gx = flux(e, inv, pres, 0)
    for f in range(8):
        out[f] = out[f] + edges(0.5 * lanes_along(gx[f], e[f]))

    pl.when(edge)(swap.wait_send)


def solution(mesh):
    n_az, n_rad = mesh.shape["az"], mesh.shape["rad"]

    def shards(density, momentum, magnetic, tracer, shear_offset):
        half = n_az // 2 * density.shape[1]
        f32 = jnp.float32
        anywhere = pl.BlockSpec(memory_space=pl.ANY)
        return pl.pallas_call(
            functools.partial(kernel, n_az, n_rad, 12 if n_az % 12 == 0 else 2, half),
            out_shape=pltpu.VMEM((8, 4, 16, 128), f32),
            in_specs=[anywhere] * 5,
            out_specs=pl.BlockSpec(memory_space=pltpu.VMEM),
            scratch_shapes=[
                pltpu.SMEM((2,), jnp.int32),
                pltpu.VMEM((8, 4, 32, 128), f32),
                pltpu.VMEM((8, 4, 32, 128), f32),
                pltpu.VMEM((8, 4, 32, 128), f32),
                pltpu.VMEM((4, 32, 128), f32),
                pltpu.VMEM((2, 8, 128), f32),
                pltpu.VMEM((2, 8, 128), f32),
                pltpu.VMEM((2, 8, 128), f32),
                pltpu.VMEM((2, 48, 128), f32),
                pltpu.VMEM((2, 48, 128), f32),
                pltpu.VMEM((64, 128), f32),
                pltpu.VMEM((24, 32, 128), f32),
                pltpu.VMEM((16, 128), f32),
                pltpu.VMEM((16, 128), f32),
                pltpu.SemaphoreType.DMA((2,)),
                pltpu.SemaphoreType.DMA((6,)),
                pltpu.SemaphoreType.DMA((7,)),
                pltpu.SemaphoreType.REGULAR,
            ],
            compiler_params=pltpu.CompilerParams(collective_id=0, has_side_effects=True),
        )(shear_offset, density, momentum, magnetic, tracer)

    placed = (
        P(None, "az", "rad"),
        P(None, None, "az", "rad"),
        P(None, None, "az", "rad"),
        P(None, "az", "rad"),
        P(),
    )
    return jax.shard_map(
        shards, mesh=mesh, in_specs=placed, out_specs=P(None, None, "az", "rad"), check_vma=False
    )
```

```python
import functools

import jax
import jax.numpy as jnp
from jax import lax
from jax.experimental import pallas as pl
from jax.experimental.pallas import tpu as pltpu
from jax.sharding import PartitionSpec as P

time_step = 0.025
viscosity = 0.5
sound_squared = 1.0
shear_speed = 1.0
frac_weight = 0.375

MESH = pl.DeviceIdType.MESH
D1 = -time_step * 45.0 / 60.0
D2 = time_step * 9.0 / 60.0
D3 = -time_step / 60.0
VISC = time_step * viscosity
lead = 1.0 - frac_weight
trail = frac_weight

S_MAIN, S_CORNER, S_FULL, S_AZ, S_Y, S_SWAP = range(6)
R_LEFT, R_RIGHT, R_FULL, R_AZ, R_PREV, R_NEXT, R_SWAP = range(7)


def flux(q, inv, pres, d):
    vel = [q[1 + i] * inv for i in range(3)]
    mag = q[4:7]
    vd, bd = vel[d], mag[d]
    out = [q[1 + d]]
    for i in range(3):
        g = q[1 + i] * vd - mag[i] * bd
        out.append(g + pres if i == d else g)
    for i in range(3):
        out.append(vd * mag[i] - bd * vel[i])
    out.append(q[7] * vd)
    return out


def aux(q):
    inv = 1.0 / q[0]
    pres = sound_squared * q[0] + 0.5 * (q[4] * q[4] + q[5] * q[5] + q[6] * q[6])
    return inv, pres


def combine(up, down):
    return D1 * (up[0] - down[0]) + D2 * (up[1] - down[1]) + D3 * (up[2] - down[2])


def lane_roll(x, shift):
    shift %= 128
    return x if shift == 0 else pltpu.roll(x, shift, x.ndim - 1)


def lanes_along(g, u):
    r = combine([lane_roll(g, -k) for k in (1, 2, 3)], [lane_roll(g, k) for k in (1, 2, 3)])
    return r + VISC * (lane_roll(u, -1) - 2.0 * u + lane_roll(u, 1))


def around(x, k):
    k %= x.shape[0]
    return x if k == 0 else jnp.concatenate([x[k:], x[:k]], axis=0)


def layers_along(g, u):
    r = combine([around(g, k) for k in (1, 2, 3)], [around(g, -k) for k in (1, 2, 3)])
    return r + VISC * (around(u, 1) - 2.0 * u + around(u, -1))


def lane_layers_along(g, u):
    r = combine([lane_roll(g, -32 * k) for k in (1, 2, 3)], [lane_roll(g, 32 * k) for k in (1, 2, 3)])
    return r + VISC * (lane_roll(u, -32) - 2.0 * u + lane_roll(u, 32))


def edge_lanes(lane):
    return jnp.logical_or(lane < 3, lane >= 125)


def edges(strip_f, lane):
    cols = lane % 32
    joined = jnp.where(jnp.logical_and(cols >= 5, cols < 8), lane_roll(strip_f, -16), strip_f)
    return jnp.stack([jnp.where(edge_lanes(lane), lane_roll(joined, -(32 * z + 8)), 0.0) for z in range(4)])


def finish(pre, part, result, buf, sem):
    lane = lax.broadcasted_iota(jnp.int32, (1, 128), 1)
    copies = [pltpu.make_async_copy(buf.at[f], result.at[f], sem) for f in range(8)]
    for f in range(8):
        buf[f] = pre[f] + edges(part[f], lane)
        if f:
            copies[f - 1].start()
    copies[7].start()
    pltpu.make_async_copy(buf, result, sem).wait()


def kernel(n_az, n_rad, run, half_offset, off_hbm, den, mom, mag, tra, out, part,
           off_ref, w, s1, fy, own, far, far_l, far_r, bhl, bhr, az, es, sp, sq, in_sem, send, recv, go):
    a = lax.axis_index("az")
    r = lax.axis_index("rad")
    first = r == 0
    last = r == n_rad - 1
    edge = jnp.logical_or(first, last)
    r_up = lax.rem(r + 1, n_rad)
    r_dn = lax.rem(r + n_rad - 1, n_rad)

    def at(step):
        return lax.rem(a + step + n_az, n_az)

    def dev(step, to_r):
        return (at(step), to_r)

    rows = pl.ds(8, 16)
    loads = [pltpu.make_async_copy(den, w.at[0, :, rows], in_sem.at[0])]
    for i in range(3):
        loads.append(pltpu.make_async_copy(mom.at[i], w.at[1 + i, :, rows], in_sem.at[0]))
        loads.append(pltpu.make_async_copy(mag.at[i], w.at[4 + i, :, rows], in_sem.at[0]))
    loads.append(pltpu.make_async_copy(tra, w.at[7, :, rows], in_sem.at[0]))
    offsets = pltpu.make_async_copy(off_hbm, off_ref, in_sem.at[1])
    for c in loads:
        c.start()
    offsets.start()

    barrier = pltpu.get_barrier_semaphore()

    def greet(step, to_r):
        pl.semaphore_signal(barrier, inc=1, device_id=dev(step, to_r), device_id_type=MESH)

    even = lax.rem(r, 2) == 0
    odd = jnp.logical_not(even)
    place = lax.rem(a, run)
    head, tail = place == 0, place == run - 1
    odd_head, odd_tail = jnp.logical_and(odd, head), jnp.logical_and(odd, tail)

    @pl.when(even)
    def _():
        for step in (-1, 0, 1):
            greet(step, r_up)
            greet(step, r_dn)

    @pl.when(first)
    def _():
        greet(2, r_dn)

    greets_half = jnp.logical_or(first, jnp.logical_and(last, head))
    told = jnp.logical_and(last, jnp.logical_not(head))

    @pl.when(greets_half)
    def _():
        greet(n_az // 2, r)

    @pl.when(jnp.logical_or(even, jnp.logical_not(tail)))
    def _():
        greet(1, r)

    @pl.when(jnp.logical_or(even, head))
    def _():
        greet(-1, r)

    w[:, :, 0:2, :] = jnp.ones((8, 4, 2, 128), jnp.float32)
    w[:, :, 30:32, :] = jnp.ones((8, 4, 2, 128), jnp.float32)
    block = w.at[:, :, rows]
    pltpu.make_async_copy(block, block, in_sem.at[0]).wait()

    lane = lax.broadcasted_iota(jnp.int32, (1, 128), 1)
    group = lane // 4
    slot_is = [lane % 32 // 4 == k for k in range(8)]
    left_half = lane % 32 < 16

    def pack(read, count):
        tiles = [jnp.zeros((count, 128), jnp.float32)] * 4
        for f in range(8):
            x = read(f)
            for z in range(4):
                moved = lane_roll(x[z], 32 * z + 4 * f)
                for t, shift in enumerate((0, 1, -1, -2)):
                    here = group == (8 * z + f + shift) % 32
                    tiles[t] = jnp.where(here, moved, tiles[t])
        return tiles

    def spread(f, hlf, hln, ln, lf, rf, rn, hrn, hrf):
        def of(k):
            return slot_is[(f + k) % 8]
        left = jnp.where(of(-2), hlf, jnp.where(of(-1), hln, jnp.where(of(0), ln, lf)))
        right = jnp.where(of(-2), rf, jnp.where(of(-1), rn, jnp.where(of(0), hrn, hrf)))
        return jnp.where(left_half, lane_roll(left, 4 * (2 - f)), lane_roll(right, 4 * (6 - f)))

    tiles = pack(lambda f: w[f, :, 8:24, :], 16)
    for t in range(4):
        own[t, 8:24, :] = tiles[t]
    inner_two = lane % 4 < 2
    far[0] = jnp.where(inner_two, tiles[1][0:8], lane_roll(tiles[1][8:16], 2))
    far[1] = jnp.where(inner_two, lane_roll(tiles[3][8:16], -2), tiles[3][0:8])
    az[24:40, :] = jnp.where(first, tiles[0], tiles[2])

    one = jnp.int32(1)
    zero = jnp.int32(0)
    along = jnp.where(even, 2 * one, jnp.where(head, zero, jnp.where(tail, 2 * one, one)))
    across = jnp.where(even, zero, jnp.where(last, 7 * one, 6 * one))
    pl.semaphore_wait(barrier, along + across + jnp.where(greets_half, one, zero))

    def remote(k, n, src, dst, step, to_r):
        return pltpu.make_async_remote_copy(
            src_ref=src, dst_ref=dst, send_sem=send.at[k], recv_sem=recv.at[n],
            device_id=dev(step, to_r), device_id_type=MESH)

    def arrived(ref, sem):
        pltpu.make_async_copy(ref, ref, sem).wait()

    own_l, own_r = own.at[0, 8:24], own.at[2, 8:24]
    ln, rn = own.at[0], own.at[2]
    hl_main = (remote(S_MAIN, R_LEFT, own_r, bhl.at[0, 8:24], 0, r_up),
               remote(S_MAIN, R_LEFT, far.at[1], far_l.at[0], 0, r_up))
    hr_main = (remote(S_MAIN, R_RIGHT, own_l, bhr.at[0, 24:40], 0, r_dn),
               remote(S_MAIN, R_RIGHT, far.at[0], far_r.at[0], 0, r_dn))
    hl_full = (remote(S_FULL, R_FULL, own_r, bhl.at[0, 24:40], -1, r_up),
               remote(S_FULL, R_FULL, far.at[1], far_l.at[1], -1, r_up))
    hr_full = (remote(S_FULL, R_FULL, own_l, bhr.at[0, 8:24], 1, r_dn),
               remote(S_FULL, R_FULL, far.at[0], far_r.at[1], 1, r_dn))
    hl_prev = remote(S_CORNER, R_LEFT, rn.at[21:24], bhl.at[0, 5:8], 1, r_up)
    hr_next = remote(S_CORNER, R_RIGHT, ln.at[8:11], bhr.at[0, 40:43], -1, r_dn)
    hl_next_in = remote(S_CORNER, R_LEFT, rn.at[8:11], bhl.at[0, 24:27], -1, r_up)
    hl_next_end = remote(S_CORNER, R_LEFT, rn.at[8:11], bhl.at[0, 40:43], -2, r_up)
    hr_prev_in = remote(S_CORNER, R_RIGHT, ln.at[21:24], bhr.at[0, 21:24], 1, r_dn)
    hr_prev_end = remote(S_CORNER, R_RIGHT, ln.at[21:24], bhr.at[0, 5:8], 2, r_dn)
    az_prev = remote(S_AZ, R_AZ, az.at[24:40], az.at[8:24], 1, r)
    az_next = remote(S_AZ, R_AZ, az.at[24:40], az.at[40:56], -1, r)
    y_prev = remote(S_Y, R_PREV, w.at[:, :, 18:24], w.at[:, :, 2:8], 1, r)
    y_next = remote(S_Y, R_NEXT, w.at[:, :, 8:14], w.at[:, :, 24:30], -1, r)
    swap = remote(S_SWAP, R_SWAP, sp, sq, n_az // 2, r)

    def send_right():
        for c in hl_main:
            c.start()

        @pl.when(last)
        def _():
            for c in hl_full:
                c.start()
            hl_next_end.start()

        @pl.when(jnp.logical_not(last))
        def _():
            hl_next_in.start()

        hl_prev.start()

    def send_left():
        for c in hr_main:
            c.start()

        @pl.when(first)
        def _():
            for c in hr_full:
                c.start()
            hr_prev_end.start()

        @pl.when(jnp.logical_not(first))
        def _():
            hr_prev_in.start()

        hr_next.start()

    def send_up():
        @pl.when(edge)
        def _():
            az_prev.start()
        y_prev.start()

    def send_down():
        @pl.when(edge)
        def _():
            az_next.start()
        y_next.start()

    @pl.when(odd)
    def _():
        send_right()
        send_left()
        arrived(az.at[0:48], send.at[S_MAIN])

    pl.when(jnp.logical_or(even, tail))(send_up)
    pl.when(jnp.logical_not(odd_head))(send_down)

    @pl.when(jnp.logical_and(odd, jnp.logical_not(tail)))
    def _():
        y_next.wait_recv()
        send_up()

    @pl.when(odd_head)
    def _():
        y_prev.wait_recv()
        send_down()

    @pl.when(jnp.logical_or(even, tail))
    def _():
        y_next.wait_recv()

    @pl.when(jnp.logical_not(odd_head))
    def _():
        y_prev.wait_recv()

    cols = lane % 32

    edge_lane = edge_lanes(lane)

    low = pack(lambda f: w[f, :, 0:8, :], 8)
    high = pack(lambda f: w[f, :, 24:32, :], 8)
    for t in range(4):
        own[t, 0:8, :] = low[t]
        own[t, 24:32, :] = high[t]
    q = [w[f] for f in range(8)]
    inv, pres = aux(q)
    gy = flux(q, inv, pres, 1)
    for f in range(8):
        fy[f] = gy[f]
    q = [w[f, :, 5:29, :] for f in range(8)]
    inv, pres = aux(q)
    gx = flux(q, inv, pres, 0)
    gz = flux(q, inv, pres, 2)
    for f in range(8):
        def y(k, f=f):
            return fy[f, :, 5 + k:29 + k, :]
        ty = combine([y(1), y(2), y(3)], [y(-1), y(-2), y(-3)])
        ty = ty + VISC * (w[f, :, 6:30, :] - 2.0 * q[f] + w[f, :, 4:28, :])
        tx = jnp.where(edge_lane, 0.0, lanes_along(gx[f], q[f]))
        s1[f, :, 0:24, :] = q[f] + tx + ty + layers_along(gz[f], q[f])

    offsets.wait()
    s_raw = jnp.clip(off_ref[0], 0, 15)
    t_raw = jnp.clip(off_ref[1] - half_offset, 0, 15)
    s_f = jnp.where(first, s_raw, zero)
    s_l = jnp.where(last, s_raw, zero)
    t_f = jnp.where(first, t_raw, zero)
    t_l = jnp.where(last, t_raw, zero)
    end_l = jnp.where(last, 1, zero)
    end_f = jnp.where(first, 1, zero)

    arrived(az.at[0:30], recv.at[R_RIGHT])

    @pl.when(last)
    def _():
        arrived(az.at[0:24], recv.at[R_FULL])

    pl.when(even)(send_right)
    arrived(az.at[0:30], recv.at[R_LEFT])

    @pl.when(first)
    def _():
        arrived(az.at[0:24], recv.at[R_FULL])

    pl.when(even)(send_left)

    @pl.when(edge)
    def _():
        arrived(az.at[0:32], recv.at[R_AZ])

    def jump(fields, mask_l, mask_r):
        add = jnp.where(mask_l, shear_speed, 0.0) - jnp.where(mask_r, shear_speed, 0.0)
        fields[2] = jnp.where(jnp.logical_or(mask_l, mask_r), fields[2] + add * fields[0], fields[2])

    win = 24
    for k, row in ((0, 8), (1, 24)):
        bhl[1, row:row + 8, :] = far_l[k]
        bhl[1, row + 8:row + 16, :] = lane_roll(far_l[k], 2)
        bhr[1, 32 - row:40 - row, :] = far_r[k]
        bhr[1, 40 - row:48 - row, :] = lane_roll(far_r[k], -2)
    hlf = bhl[1, pl.ds(5 + t_f, win), :]
    hln = bhl[0, pl.ds(5 + t_f, win), :]
    hrf = bhr[1, pl.ds(21 - t_l - end_l, win), :]
    hrn = bhr[0, pl.ds(21 - t_l - end_l, win), :]
    o_l = 21 + t_f - s_f
    ln2 = jnp.where(first, trail * az[pl.ds(o_l - end_f, win), :] + lead * az[pl.ds(o_l, win), :], own[0, 5:29, :])
    o_r = 21 - t_l - end_l + s_l
    rn2 = jnp.where(last, lead * az[pl.ds(o_r, win), :] + trail * az[pl.ds(o_r + 1, win), :], own[2, 5:29, :])
    e = [spread(f, hlf, hln, ln2, ln2, rn2, rn2, hrn, hrf) for f in range(8)]
    in_l = jnp.logical_and(cols >= 8, cols < 16)
    in_r = jnp.logical_and(cols >= 16, cols < 24)
    jump(e, jnp.logical_and(last, in_r), jnp.logical_and(first, in_l))
    inv, pres = aux(e)
    gx = flux(e, inv, pres, 0)
    gy = flux(e, inv, pres, 1)
    gz = flux(e, inv, pres, 2)
    for f in range(8):
        es[f, 0:24, :] = gy[f]
    for f in range(8):
        es[8 + f, 0:24, :] = e[f]
    strip = []
    for f in range(8):
        def y(k, f=f):
            return es[f, 3 + k:20 + k, :]
        def u(k, f=f):
            return es[8 + f, 3 + k:20 + k, :]
        ty = combine([y(1), y(2), y(3)], [y(-1), y(-2), y(-3)]) + VISC * (u(1) - 2.0 * u(0) + u(-1))
        es[16 + f, 0:24, :] = e[f] + lanes_along(gx[f], e[f]) + lane_layers_along(gz[f], e[f])
        es[16 + f, 3:20, :] = es[16 + f, 3:20, :] + ty
    at_l = jnp.logical_and(first, left_half)
    at_r = jnp.logical_and(last, jnp.logical_not(left_half))
    w_0 = jnp.where(left_half, lead, trail)
    w_1 = jnp.where(left_half, trail, lead)
    sheared = jnp.logical_or(at_l, at_r)
    for f in range(8):
        here, beyond = es[16 + f, 3:19, :], es[16 + f, 4:20, :]
        strip.append(jnp.where(sheared, w_0 * here + w_1 * beyond, here))
    jump(strip, at_l, at_r)
    packed = jnp.zeros((16, 128), jnp.float32)
    for f in range(8):
        src = jnp.where(first, strip[f], lane_roll(strip[f], -20))
        packed = jnp.where(slot_is[f], lane_roll(src, 4 * (f - 1)), packed)
    sp[...] = packed

    @pl.when(told)
    def _():
        pl.semaphore_wait(go, 1)

    @pl.when(edge)
    def _():
        swap.start()

    for f in range(8):
        es[16 + f, 0:16, :] = strip[f]

    hln0, hln1 = bhl[0, pl.ds(5 + s_f, win), :], bhl[0, pl.ds(5 + s_f + end_f, win), :]
    hln = jnp.where(first, lead * hln0 + trail * hln1, hln0)
    o_r = 21 - s_l
    hrn0, hrn1 = bhr[0, pl.ds(o_r - end_l, win), :], bhr[0, pl.ds(o_r, win), :]
    hrn = jnp.where(last, trail * hrn0 + lead * hrn1, hrn1)
    mine = [own[t, 5:29, :] for t in range(4)]
    e = [spread(f, hln, hln, mine[0], mine[1], mine[3], mine[2], hrn, hrn) for f in range(8)]
    jump(e, jnp.logical_and(first, cols < 8), jnp.logical_and(last, cols >= 24))
    inv, pres = aux(e)
    gx = flux(e, inv, pres, 0)
    for f in range(8):
        s1[f, :, 0:24, :] = s1[f, :, 0:24, :] + edges(lanes_along(gx[f], e[f]), lane)

    q = [s1[f, :, 0:24, :] for f in range(8)]
    inv, pres = aux(q)
    gy = flux(q, inv, pres, 1)
    for f in range(8):
        fy[f, :, 0:24, :] = gy[f]
    q = [s1[f, :, 3:19, :] for f in range(8)]
    inv, pres = aux(q)
    gx = flux(q, inv, pres, 0)
    gz = flux(q, inv, pres, 2)
    tiles = pack(lambda f: q[f], 16)
    for f in range(8):
        def y(k, f=f):
            return fy[f, :, 3 + k:19 + k, :]
        ty = combine([y(1), y(2), y(3)], [y(-1), y(-2), y(-3)])
        ty = ty + VISC * (s1[f, :, 4:20, :] - 2.0 * q[f] + s1[f, :, 2:18, :])
        tx = jnp.where(edge_lane, 0.0, lanes_along(gx[f], q[f]))
        out[f] = 0.5 * w[f, :, 8:24, :] + 0.5 * (q[f] + tx + ty + layers_along(gz[f], q[f]))
    own_cols = jnp.logical_and(cols >= 8, cols < 24)
    for f in range(8):
        mid = spread(f, tiles[0], tiles[0], tiles[0], tiles[1], tiles[3], tiles[2], tiles[2], tiles[2])
        es[16 + f, 0:16, :] = jnp.where(own_cols, mid, es[16 + f, 0:16, :])

    @pl.when(even)
    def _():
        arrived(az.at[0:48], send.at[S_MAIN])

    arrived(az.at[0:12], send.at[S_CORNER])
    arrived(w.at[:, :, 0:12], send.at[S_Y])

    @pl.when(edge)
    def _():
        arrived(az.at[0:24], send.at[S_FULL])
        arrived(az.at[0:32], send.at[S_AZ])
        swap.wait_recv()

    @pl.when(jnp.logical_and(first, jnp.logical_not(head)))
    def _():
        pl.semaphore_signal(go, inc=1, device_id=(a, r_dn), device_id_type=MESH)

    got = sq[...]
    got = jnp.where(last, lane_roll(got, 20), got)
    theirs = jnp.logical_or(jnp.logical_and(first, cols < 8), jnp.logical_and(last, cols >= 24))
    e = [jnp.where(theirs, lane_roll(got, 4 * (1 - f)), es[16 + f, 0:16, :]) for f in range(8)]
    inv, pres = aux(e)
    gx = flux(e, inv, pres, 0)
    for f in range(8):
        part[f] = 0.5 * lanes_along(gx[f], e[f])

    pl.when(edge)(swap.wait_send)


def solution(mesh):
    n_az, n_rad = mesh.shape["az"], mesh.shape["rad"]

    def shards(density, momentum, magnetic, tracer, shear_offset):
        half = n_az // 2 * density.shape[1]
        f32 = jnp.float32
        anywhere = pl.BlockSpec(memory_space=pl.ANY)
        vmem = pl.BlockSpec(memory_space=pltpu.VMEM)
        pre, part = pl.pallas_call(
            functools.partial(kernel, n_az, n_rad, 12 if n_az % 12 == 0 else 2, half),
            out_shape=(pltpu.VMEM((8, 4, 16, 128), f32), pltpu.VMEM((8, 16, 128), f32)),
            in_specs=[anywhere] * 5,
            out_specs=(vmem, vmem),
            scratch_shapes=[
                pltpu.SMEM((2,), jnp.int32),
                pltpu.VMEM((8, 4, 32, 128), f32),
                pltpu.VMEM((8, 4, 32, 128), f32),
                pltpu.VMEM((8, 4, 32, 128), f32),
                pltpu.VMEM((4, 32, 128), f32),
                pltpu.VMEM((2, 8, 128), f32),
                pltpu.VMEM((2, 8, 128), f32),
                pltpu.VMEM((2, 8, 128), f32),
                pltpu.VMEM((2, 48, 128), f32),
                pltpu.VMEM((2, 48, 128), f32),
                pltpu.VMEM((64, 128), f32),
                pltpu.VMEM((24, 32, 128), f32),
                pltpu.VMEM((16, 128), f32),
                pltpu.VMEM((16, 128), f32),
                pltpu.SemaphoreType.DMA((2,)),
                pltpu.SemaphoreType.DMA((6,)),
                pltpu.SemaphoreType.DMA((7,)),
                pltpu.SemaphoreType.REGULAR,
            ],
            compiler_params=pltpu.CompilerParams(collective_id=0, has_side_effects=True),
        )(shear_offset, density, momentum, magnetic, tracer)
        return pl.pallas_call(
            finish,
            out_shape=jax.ShapeDtypeStruct((8, 4, 16, 128), f32),
            in_specs=[vmem, vmem],
            out_specs=anywhere,
            scratch_shapes=[pltpu.VMEM((8, 4, 16, 128), f32), pltpu.SemaphoreType.DMA],
        )(*[pltpu.with_memory_space_constraint(q, pltpu.VMEM) for q in (pre, part)])

    placed = (
        P(None, "az", "rad"),
        P(None, None, "az", "rad"),
        P(None, None, "az", "rad"),
        P(None, "az", "rad"),
        P(),
    )
    return jax.shard_map(
        shards, mesh=mesh, in_specs=placed, out_specs=P(None, None, "az", "rad"), check_vma=False
    )
```
